32 devices in a mesh: groups: 2 (over x), gx: 4 (over y, core), gy: 4 (over z).
Axes of the slice: x: 2, y: 2, z: 4, core: 2. Of those that a mesh axis runs over, the one named last changes fastest.
Arguments:
- tokens: bfloat16 [64, 2, 16384], P('groups', None, 'gx'), parts along dimension 0
- norm_gain: bfloat16 [16384], P('gx'), may hold values from 0.099609375 to 1.8984375
- qkv_weight: bfloat16 [16384, 8, 18, 128], P('gx', 'gy'), may hold values from -0.046875 to 0.046875
- out_weight: bfloat16 [128, 128, 16384], P('gy', None, 'gx'), may hold values from -0.125 to 0.125
- kv_cache: bfloat16 [64, 384, 2, 8, 128], P(('groups', 'gx', 'gy')), parts along dimension 0
- lengths: int32 [64], P(('groups', 'gx', 'gy')), parts along dimension 0, may hold values from 1 to 384, as said below
- positions: int32 [64], P('groups'), parts along dimension 0, may hold values from 0 to 4095
Outputs:
- layer_out: float32 [64, 2, 16384], P(('groups', 'gy'), None, 'gx'), parts along dimension 0
The draws below stay inside these ranges and needn't reach their ends.
There are 2 independent parts, one for each index of `groups`. The reference program is written for one: setup_inputs(seed, part) draws one part's arguments, and reference() takes and returns one part's arrays. A program takes and returns all parts, laid end to end along the dimension named above; an argument that names none is the same for every part. Nothing has to cross between parts.
Inputs may be any that keep to these rules, and one draw needn't show every extreme that they name: Cache slots 0 to lengths - 1 of a row hold its earlier tokens; some row has exactly 384.
All inputs are finite; a program needn't handle non-finite values.
Results may differ from the reference program's by a relative error of at most 0.025.
Values may be sent and summed in bfloat16 or wider, within the bound.
A program may use at most 192 MiB of HBM per device.

```python
import math
import jax
import jax.numpy as jnp
from jax import lax

D = 16384
HQ = 128
KV = 8
HD = 128
GQ = 16
MAXLEN = 384
ROWS = 32


def draw_tokens(key, part):
    key_base = jax.random.fold_in(key, 11)
    noise_key, scale_key = jax.random.split(key_base)
    columns = jnp.arange(D, dtype=jnp.float32) / D
    noise_part = jax.random.normal(noise_key, (ROWS, 2, D), jnp.float32)
    column_scale = jnp.exp(columns * jnp.log(10.0)) / 3.2
    row_scale = jnp.exp(jax.random.uniform(scale_key, (ROWS, 2, 1), jnp.float32, -0.7, 0.7))
    return (noise_part * column_scale * row_scale).astype(jnp.bfloat16)


def draw_kv_cache(key, part):
    key_base = jax.random.fold_in(key, 23)
    value_key = jax.random.fold_in(key_base, 0)
    entries = jax.random.normal(value_key, (ROWS, MAXLEN, 2, KV, HD), jnp.float32)
    return entries.astype(jnp.bfloat16)


def draw_lengths(key, part):
    key_base = jax.random.fold_in(key, 37)
    long_key, short_key, pick_key, top_key = jax.random.split(key_base, 4)
    long_draw = jax.random.randint(long_key, (ROWS,), 1, MAXLEN + 1)
    short_draw = jax.random.randint(short_key, (ROWS,), 1, MAXLEN // 16 + 2)
    picker = jax.random.randint(pick_key, (ROWS,), 0, 4)
    chosen = jnp.where(picker == 0, short_draw, long_draw)
    top_row = jax.random.randint(top_key, (), 0, ROWS)
    chosen = jnp.where(jnp.arange(ROWS, dtype=jnp.int32) == top_row, MAXLEN, chosen)
    return chosen.astype(jnp.int32)


def place_ends(drawn, stream_key, low, largest):
    longest = drawn.shape.index(max(drawn.shape))
    spots = []
    for shift in (0, 1):
        where = [jax.random.randint(jax.random.fold_in(stream_key, axis), (), 0, length) for axis, length in enumerate(drawn.shape)]
        where[longest] = (where[longest] + shift) % drawn.shape[longest]
        spots.append(tuple(where))
    return drawn.at[spots[0]].set(low).at[spots[1]].set(largest)


def levels(stream_key, dims, pieces, smallest, top_value):
    def one(axis_at, blocks):
        steps = jax.random.uniform(jax.random.fold_in(jax.random.fold_in(stream_key, 6), axis_at), (blocks,), jnp.float32, smallest / len(pieces), top_value / len(pieces))
        return jnp.repeat(jnp.exp(steps), dims[axis_at] // blocks).reshape((-1,) + (1,) * (len(dims) - axis_at - 1))

    level = one(*pieces[0])
    for cut in pieces[1:]:
        level = level * one(*cut)
    return level


def bell_draw(stream_key, dims, scale, most, cuts=(), kind=jnp.bfloat16):
    loudness = levels(stream_key, dims, cuts, -0.22, 0.18) if cuts else 1.0
    array = jax.random.normal(stream_key, dims, jnp.float32) * scale * loudness
    return jnp.minimum(jnp.maximum(array, -most), most).astype(kind)


def setup_inputs(seed: int = 0, part: int = 0) -> dict:
    key_of = jax.random.split(jax.random.key(seed), 8)
    part_keys = jax.random.split(jax.random.fold_in(key_of[7], part), 8)
    tokens = draw_tokens(jax.random.fold_in(jax.random.fold_in(key_of[7], part), 71), part)
    norm_gain = jnp.clip(1.0 + 0.18 * jax.random.normal(key_of[1], (D,), jnp.float32), 0.099609375, 1.8984375).astype(jnp.bfloat16)
    qkv_weight = bell_draw(key_of[2], (D, KV, GQ + 2, HD), D ** -0.5, 0.046875, ((0, 4), (1, 4)))
    out_weight = bell_draw(key_of[3], (HQ, HD, D), (GQ * HD) ** -0.5, 0.125, ((0, 4), (2, 4)))
    kv_cache = draw_kv_cache(jax.random.fold_in(jax.random.fold_in(key_of[7], part), 71), part)
    lengths = draw_lengths(jax.random.fold_in(jax.random.fold_in(key_of[7], part), 71), part)
    positions = place_ends(jax.random.randint(part_keys[6], (ROWS,), 0, 4096), jax.random.fold_in(part_keys[6], 1), 0, 4095).astype(jnp.int32)
    return dict(tokens=tokens, norm_gain=norm_gain, qkv_weight=qkv_weight, out_weight=out_weight, kv_cache=kv_cache, lengths=lengths, positions=positions)


norm_eps = 1e-05
rope_base = 500000.0

def rotate(values, places):
    half_dim = values.shape[-1] // 2
    index_half = jnp.arange(half_dim, dtype=jnp.float32)
    frequency = rope_base ** (-2.0 * index_half / values.shape[-1])
    angles = places[..., None] * frequency
    cosine = jnp.cos(angles)
    sine_part = jnp.sin(angles)
    front_half = values[..., :half_dim]
    back_half = values[..., half_dim:]
    return jnp.concatenate([front_half * cosine - back_half * sine_part, back_half * cosine + front_half * sine_part], axis=-1)

def attend(queries, key_new, value_new, cache_rows, length):
    scale_factor = 1.0 / math.sqrt(queries.shape[-1])
    query_wide = queries.astype(jnp.float32)
    old_keys = cache_rows[:, :, 0].astype(jnp.float32)
    old_values = cache_rows[:, :, 1].astype(jnp.float32)
    scores_old = jnp.einsum('rtgid,rsgd->rtgis', query_wide, old_keys) * scale_factor
    slot_ids = jnp.arange(cache_rows.shape[1], dtype=jnp.int32)
    visible = slot_ids[None, :] < length[:, None]
    scores_old = jnp.where(visible[:, None, None, None, :], scores_old, -1e+30)
    scores_new = jnp.einsum('rtgid,rugd->rtgiu', query_wide, key_new.astype(jnp.float32)) * scale_factor
    token_ids = jnp.arange(queries.shape[1], dtype=jnp.int32)
    causal = token_ids[:, None] >= token_ids[None, :]
    scores_new = jnp.where(causal[None, :, None, None, :], scores_new, -1e+30)
    highest = jnp.maximum(lax.optimization_barrier(jnp.max(scores_old, axis=-1)), lax.optimization_barrier(jnp.max(scores_new, axis=-1)))
    expo_old = jnp.exp(scores_old - highest[..., None])
    expo_new = jnp.exp(scores_new - highest[..., None])
    denominator = lax.optimization_barrier(jnp.sum(expo_old, axis=-1)) + lax.optimization_barrier(jnp.sum(expo_new, axis=-1))
    weight_old = (expo_old / denominator[..., None]).astype(jnp.bfloat16)
    weight_new = (expo_new / denominator[..., None]).astype(jnp.bfloat16)
    attended = jnp.einsum('rtgis,rsgd->rtgid', weight_old.astype(jnp.float32), old_values)
    attended = attended + jnp.einsum('rtgiu,rugd->rtgid', weight_new.astype(jnp.float32), value_new.astype(jnp.float32))
    return attended.astype(jnp.bfloat16)

def reference(tokens, norm_gain, qkv_weight, out_weight, kv_cache, lengths, positions):
    tokens_wide = tokens.astype(jnp.float32)
    hidden = (tokens_wide * norm_gain.astype(jnp.float32)).astype(jnp.bfloat16)
    inv_rms = lax.rsqrt(lax.optimization_barrier(jnp.sum(tokens_wide * tokens_wide, axis=-1)) / D + norm_eps)
    projected = jnp.dot(hidden.reshape(ROWS * 2, D), qkv_weight.reshape(D, KV * (GQ + 2) * HD), preferred_element_type=jnp.float32)
    projected = projected.reshape(ROWS, 2, KV, GQ + 2, HD) * inv_rms[:, :, None, None, None]
    places = (positions[:, None] + jnp.arange(2, dtype=jnp.int32)[None, :]).astype(jnp.float32)
    queries = rotate(projected[:, :, :, :GQ], places[:, :, None, None]).astype(jnp.bfloat16)
    key_new = rotate(projected[:, :, :, GQ], places[:, :, None]).astype(jnp.bfloat16)
    value_new = projected[:, :, :, GQ + 1].astype(jnp.bfloat16)

    def one_row(packed):
        return attend(packed[0], packed[1], packed[2], packed[3], packed[4])
    attended = lax.map(one_row, (queries[:, None], key_new[:, None], value_new[:, None], kv_cache[:, None], lengths[:, None]))
    attended = attended.reshape(ROWS * 2, HQ * HD)
    update = jnp.dot(attended, out_weight.reshape(HQ * HD, D), preferred_element_type=jnp.float32)
    return tokens_wide + update.reshape(ROWS, 2, D)
```

```python
import functools
import math

import jax
import jax.numpy as jnp
from jax import lax
from jax.experimental import pallas as pl
from jax.experimental.pallas import tpu as pltpu
from jax.sharding import PartitionSpec as P

D = 16384


norm_eps = 1e-05
rope_base = 500000.0


def rotate(values, places):
    half_dim = values.shape[-1] // 2
    index_half = jnp.arange(half_dim, dtype=jnp.float32)
    frequency = rope_base ** (-2.0 * index_half / values.shape[-1])
    angles = places[..., None] * frequency
    cosine = jnp.cos(angles)
    sine_part = jnp.sin(angles)
    front_half = values[..., :half_dim]
    back_half = values[..., half_dim:]
    return jnp.concatenate(
        [front_half * cosine - back_half * sine_part, back_half * cosine + front_half * sine_part],
        axis=-1,
    )


def finish(projected, positions, first_row, row_count):
    group_size = projected.shape[3] - 2
    placed = lax.dynamic_slice_in_dim(positions, first_row, row_count, 0)
    places = (placed[:, None] + jnp.arange(2, dtype=jnp.int32)[None, :]).astype(jnp.float32)
    queries = rotate(projected[:, :, :, :group_size], places[:, :, None, None])
    key_new = rotate(projected[:, :, :, group_size : group_size + 1], places[:, :, None, None])
    value_new = projected[:, :, :, group_size + 1 :]
    return jnp.concatenate([queries, key_new, value_new], axis=3).astype(jnp.bfloat16)


def attend(queries, key_new, value_new, cache_rows, length):
    scale_factor = 1.0 / math.sqrt(queries.shape[-1])
    scores_old = (
        jnp.einsum(
            "rtgid,rsgd->rtgis", queries, cache_rows[:, :, 0], preferred_element_type=jnp.float32
        )
        * scale_factor
    )
    slot_ids = jnp.arange(cache_rows.shape[1], dtype=jnp.int32)
    visible = slot_ids[None, :] < length[:, None]
    scores_old = jnp.where(visible[:, None, None, None, :], scores_old, -1e30)
    scores_new = (
        jnp.einsum("rtgid,rugd->rtgiu", queries, key_new, preferred_element_type=jnp.float32)
        * scale_factor
    )
    token_ids = jnp.arange(queries.shape[1], dtype=jnp.int32)
    causal = token_ids[:, None] >= token_ids[None, :]
    scores_new = jnp.where(causal[None, :, None, None, :], scores_new, -1e30)
    highest = jnp.maximum(jnp.max(scores_old, axis=-1), jnp.max(scores_new, axis=-1))
    expo_old = jnp.exp(scores_old - highest[..., None])
    expo_new = jnp.exp(scores_new - highest[..., None])
    denominator = jnp.sum(expo_old, axis=-1) + jnp.sum(expo_new, axis=-1)
    weight_old = (expo_old / denominator[..., None]).astype(jnp.bfloat16)
    weight_new = (expo_new / denominator[..., None]).astype(jnp.bfloat16)
    attended = jnp.einsum(
        "rtgis,rsgd->rtgid", weight_old, cache_rows[:, :, 1], preferred_element_type=jnp.float32
    )
    attended = attended + jnp.einsum(
        "rtgiu,rugd->rtgid", weight_new, value_new, preferred_element_type=jnp.float32
    )
    return attended.astype(jnp.bfloat16)


def hop(source, target, sends, arrivals, place):
    return pltpu.make_async_remote_copy(
        src_ref=source,
        dst_ref=target,
        send_sem=sends,
        recv_sem=arrivals,
        device_id=place,
        device_id_type=pl.DeviceIdType.MESH,
    )


def block_kernel(
    head_devices,
    places,
    tokens_ref,
    gain_ref,
    qkv_ref,
    out_weight_ref,
    cache_ref,
    lengths_ref,
    positions_ref,
    out_ref,
    raw,
    tok,
    gain,
    gain_wide,
    left,
    ring,
    chunk,
    weights,
    own_sum,
    core_send,
    core_recv,
    row_send,
    row_recv,
    square_all,
    square_core,
    square_mid,
    square_recv,
    query_buf,
    attended_buf,
    attended_send,
    attended_recv,
    part_send,
    part_recv,
    part_own,
    load_sems,
    ring_sems,
    tile_sems,
    weight_sems,
    core_sems,
    row_sends,
    row_recvs,
    square_sems,
    att_sends,
    att_recvs,
    pair_sends,
    pair_recvs,
    part_sends,
    part_recvs,
):
    f32, bf16 = jnp.float32, jnp.bfloat16
    rows_total, pair, local_width = raw.shape
    total_tokens = rows_total * pair
    columns, head_dim = qkv_ref.shape[1], qkv_ref.shape[3]
    groups = qkv_ref.shape[2]
    group_size = columns - 2
    pieces = columns // 2
    slots = ring.shape[0]
    max_len = (cache_ref.shape[0] // (2 * groups * head_devices)) // lengths_ref.shape[0]
    rows_local = lengths_ref.shape[0]
    all_groups = groups * head_devices
    near = rows_local * pair
    block = groups * near
    lanes = places // 2
    team = lanes * head_devices
    contraction = local_width * groups
    width = lax.axis_index("gx")
    head = lax.axis_index("gy")
    core = lax.rem(width, 2)
    lane_at = width // 2
    mine = lane_at * head_devices + head
    source_at = width * head_devices + head
    partner = {"gx": width + 1 - 2 * core}

    def member(off):
        other = lax.rem(mine + off, team)
        far_lane, far_head = other // head_devices, lax.rem(other, head_devices)
        return other, {"gx": far_lane * 2 + core, "gy": far_head}

    def bring(piece, slot):
        return [
            pltpu.make_async_copy(
                qkv_ref.at[:, piece * 2 + at], ring.at[slot, at], ring_sems.at[slot, at]
            )
            for at in range(2)
        ]

    load_tokens = pltpu.make_async_copy(tokens_ref, raw, load_sems.at[0])
    load_gain = pltpu.make_async_copy(gain_ref, gain, load_sems.at[1])
    load_tokens.start()
    load_gain.start()
    for piece in range(min(slots, pieces)):
        for copy in bring(piece, piece):
            copy.start()
    barrier = pltpu.get_barrier_semaphore()
    pl.semaphore_signal(barrier, inc=1, device_id=partner, device_id_type=pl.DeviceIdType.MESH)
    for off in range(1, team):
        pl.semaphore_signal(
            barrier, inc=1, device_id=member(off)[1], device_id_type=pl.DeviceIdType.MESH
        )

    made = lax.broadcasted_iota(jnp.int32, (total_tokens * groups, total_tokens), 0)
    held = lax.broadcasted_iota(jnp.int32, (total_tokens * groups, total_tokens), 1)
    target = made // block
    owner_core = target // team
    owner_lane = lax.rem(target, team) // head_devices
    owner_head = lax.rem(target, head_devices)
    owner = (owner_lane * 2 + owner_core) * head_devices + owner_head
    chosen = owner * near + lax.rem(made, near) == held
    chooser = jnp.where(chosen, 1.0, 0.0)
    group_row = lax.rem(
        lax.broadcasted_iota(jnp.int32, (total_tokens * groups, 128), 0), block
    ) // near
    feature = lax.broadcasted_iota(jnp.int32, (128 * groups, 128 * groups), 0)
    goal = lax.broadcasted_iota(jnp.int32, (128 * groups, 128 * groups), 1)
    spread = jnp.where(
        goal == lax.rem(feature, 128) * groups + feature // 128, 1.0, 0.0
    ).astype(bf16)

    load_tokens.wait()
    retile = pltpu.make_async_copy(
        raw.reshape(total_tokens, local_width), tok, load_sems.at[2]
    )
    retile.start()
    load_gain.wait()
    gain_wide[...] = gain[...].astype(f32)
    retile.wait()
    depth = 512

    def widen(at, squares):
        start = pl.multiple_of(at * depth, depth)
        wide = tok[:, pl.ds(start, depth)].astype(f32)
        scale = jnp.concatenate(
            [gain_wide[pl.ds(at * (depth // 128) + q, 1), :] for q in range(depth // 128)], axis=1
        )
        hidden = (wide * scale).astype(bf16)
        ordered = jnp.dot(chooser.astype(bf16), hidden, preferred_element_type=f32)
        for q in range(depth // 128):
            part = wide[:, q * 128 : (q + 1) * 128]
            squares += part * part
            near_part = ordered[:, q * 128 : (q + 1) * 128]
            split = jnp.concatenate(
                [jnp.where(group_row == group, near_part, 0.0) for group in range(groups)], axis=1
            ).astype(bf16)
            begin = pl.multiple_of((start + q * 128) * groups, 128 * groups)
            left[:, pl.ds(begin, 128 * groups)] = jnp.dot(
                split, spread, preferred_element_type=f32
            ).astype(bf16)
        return squares

    squares = lax.fori_loop(
        0, local_width // depth, widen, jnp.zeros((total_tokens, 128), f32)
    )
    square_all[...] = jnp.dot(
        chooser, squares, preferred_element_type=f32, precision=lax.Precision.HIGHEST
    ).reshape(square_all.shape)
    pl.semaphore_wait(barrier, team)

    square_hop = hop(
        square_all.at[1 - core], square_core, square_sems.at[0], square_sems.at[1], partner
    )
    square_hop.start()

    def core_hop(piece):
        return hop(
            core_send.at[piece],
            core_recv.at[piece],
            core_sems.at[0, piece],
            core_sems.at[1, piece],
            partner,
        )

    def row_hop(piece, off):
        other, place = member(off)
        return hop(
            row_send.at[piece, other],
            row_recv.at[piece, mine],
            row_sends.at[piece, other],
            row_recvs.at[piece, mine],
            place,
        )

    def row_arrival(piece, off):
        other, place = member(off)
        return hop(
            row_send.at[piece, other],
            row_recv.at[piece, other],
            row_sends.at[piece, other],
            row_recvs.at[piece, other],
            place,
        )

    def pass_on(piece):
        core_hop(piece).wait_recv()
        total = own_sum[lax.rem(piece, 2), core] + core_recv[piece].astype(f32)
        row_send[piece] = total.reshape(row_send.shape[1:]).astype(bf16)
        row_recv[piece, mine] = row_send[piece, mine]
        for off in range(1, team):
            row_hop(piece, off).start()

    def weight_copy(at):
        across = part_own.shape[2]
        return pltpu.make_async_copy(
            out_weight_ref.at[:, pl.ds(at * across, across)],
            weights.at[:, pl.ds(at * across, across)],
            weight_sems.at[at],
        )

    stretches = part_own.shape[0]
    cache_slot, cached_slot = pieces % 2, (pieces - 1) % 2
    cache_rows = cache_ref.shape[0]
    load_cache = pltpu.make_async_copy(
        cache_ref, chunk.at[cache_slot, pl.ds(0, cache_rows)], load_sems.at[3]
    )

    @pl.loop(0, pieces)
    def _(piece):
        slot, here = lax.rem(piece, slots), lax.rem(piece, 2)
        for copy in bring(piece, slot):
            copy.wait()
        flat = ring.reshape(slots, 2, contraction, head_dim)
        moves = [
            pltpu.make_async_copy(
                flat.at[slot, at],
                chunk.at[here, pl.ds(at * contraction, contraction)],
                tile_sems.at[at],
            )
            for at in range(2)
        ]
        for move in moves:
            move.start()

        @pl.when(piece == pieces - 1)
        def _():
            load_cache.start()
            for at in range(stretches):
                weight_copy(at).start()

        for move in moves:
            move.wait()

        @pl.when(piece + slots < pieces)
        def _():
            for copy in bring(piece + slots, slot):
                copy.start()

        right = jnp.concatenate(
            [chunk[here, pl.ds(0, contraction)], chunk[here, pl.ds(contraction, contraction)]], axis=1
        )
        total = jnp.dot(left[...], right, preferred_element_type=f32)
        own_sum[here] = total.reshape(own_sum.shape[1:])
        core_send[piece] = own_sum[here, 1 - core].astype(bf16)
        core_hop(piece).start()

        @pl.when(piece >= 1)
        def _():
            pass_on(piece - 1)

    pass_on(pieces - 1)
    square_hop.wait_recv()
    square_mid[...] = (square_all[core] + square_core[...]).reshape(square_mid.shape)
    square_recv[lane_at] = square_mid[mine]

    def square_send(off):
        other_lane = lax.rem(lane_at + off, lanes)
        return hop(
            square_mid.at[other_lane * head_devices + head],
            square_recv.at[lane_at],
            square_sems.at[2 + 2 * off],
            square_sems.at[3 + 2 * off],
            {"gx": other_lane * 2 + core},
        )

    def square_arrival(off):
        other_lane = lax.rem(lane_at + lanes - off, lanes)
        return hop(
            square_mid.at[mine],
            square_recv.at[other_lane],
            square_sems.at[2 + 2 * off],
            square_sems.at[3 + 2 * off],
            {"gx": other_lane * 2 + core},
        )

    for off in range(1, lanes):
        square_send(off).start()

    stride = max_len + 16
    steps = 16
    kinds = 2 * all_groups
    size = steps * kinds
    to_row = lax.broadcasted_iota(jnp.int32, (size, size), 0)
    from_row = lax.broadcasted_iota(jnp.int32, (size, size), 1)
    regroup = jnp.where(
        from_row == lax.rem(to_row, steps) * kinds + to_row // steps, 1.0, 0.0
    ).astype(bf16)
    load_cache.wait()
    for row in range(rows_local):

        @pl.loop(0, max_len // (2 * steps))
        def _(step):
            first = pl.multiple_of(row * max_len * kinds + step * 2 * size, size)
            both = jnp.concatenate(
                [chunk[cache_slot, pl.ds(first, size)], chunk[cache_slot, pl.ds(first + size, size)]],
                axis=1,
            )
            sorted_rows = jnp.dot(regroup, both, preferred_element_type=f32).astype(bf16)
            for kind in range(kinds):
                base = (row * kinds + kind) * stride
                for half in range(2):
                    at = pl.multiple_of(base + (step * 2 + half) * steps, 16)
                    chunk[cached_slot, pl.ds(at, steps)] = sorted_rows[
                        kind * steps : (kind + 1) * steps, half * head_dim : (half + 1) * head_dim
                    ]

    row_at = lax.broadcasted_iota(jnp.int32, (block, head_dim), 0)
    lane = lax.broadcasted_iota(jnp.int32, (block, head_dim), 1)
    half_dim = head_dim // 2
    place = jnp.zeros((block, head_dim), jnp.int32)
    for row in range(rows_local):
        place = jnp.where(
            lax.rem(row_at, near) // pair == row, positions_ref[source_at * rows_local + row], place
        )
    place = (place + lax.rem(row_at, pair)).astype(f32)
    index_half = lax.rem(lane, half_dim).astype(f32)
    frequency = jnp.exp(index_half * (-2.0 * math.log(rope_base) / head_dim))
    angles = place * frequency
    cosine = jnp.cos(angles)
    sine = jnp.where(lane < half_dim, -jnp.sin(angles), jnp.sin(angles))

    for off in range(1, lanes):
        square_arrival(off).wait_recv()
    square_total = square_recv[0]
    for at in range(1, lanes):
        square_total = square_total + square_recv[at]
    inv_rms = lax.rsqrt(
        jnp.sum(square_total, axis=1, keepdims=True) / (local_width * places) + norm_eps
    )

    @pl.loop(0, pieces)
    def _(piece):
        for off in range(1, team):
            row_arrival(piece, off).wait_recv()

    small = lax.broadcasted_iota(jnp.int32, (block, head_dim), 0)
    for far in range(head_devices):
        for column in range(columns):
            piece, side = column // 2, column % 2
            value = row_recv[piece, far, :, side * head_dim : (side + 1) * head_dim].astype(f32)
            for at in range(1, lanes):
                value = value + row_recv[
                    piece, at * head_devices + far, :, side * head_dim : (side + 1) * head_dim
                ].astype(f32)
            value = value * inv_rms
            if column <= group_size:
                turned = jnp.concatenate([value[:, half_dim:], value[:, :half_dim]], axis=1)
                value = value * cosine + turned * sine
            if column < group_size:
                query_buf[far, column * block : (column + 1) * block, :] = value
            else:
                kind = column - group_size
                for group in range(groups):
                    for row in range(rows_local):
                        start = group * near + row * pair
                        moved = pltpu.roll(value, (block - start) % block, 0) if start else value
                        fresh = jnp.where(small < pair, moved, 0.0)
                        base = (
                            row * kinds + kind * all_groups + far * groups + group
                        ) * stride + max_len
                        chunk[cached_slot, pl.ds(base, 16)] = jnp.concatenate(
                            [fresh, jnp.zeros((16 - block, head_dim), f32)], axis=0
                        ).astype(bf16)

    scale_factor = 1.0 / math.sqrt(head_dim)
    count = pair * group_size
    slot_id = lax.broadcasted_iota(jnp.int32, (count, stride), 1)
    token_id = lax.broadcasted_iota(jnp.int32, (count, stride), 0) // group_size
    fresh_seen = (slot_id >= max_len) & (slot_id - max_len <= token_id)
    for row in range(rows_local):
        seen = (slot_id < lengths_ref[row]) | fresh_seen
        for every in range(all_groups):
            far, group = every // groups, every % groups
            first = group * near + row * pair
            queries = jnp.concatenate(
                [
                    query_buf[far, pl.ds(first + token, group_size, stride=block), :]
                    for token in range(pair)
                ],
                axis=0,
            ).astype(bf16)
            keys = chunk[cached_slot, pl.ds((row * kinds + every) * stride, stride)]
            values = chunk[cached_slot, pl.ds((row * kinds + all_groups + every) * stride, stride)]
            scores = lax.dot_general(
                queries, keys, (((1,), (1,)), ((), ())), preferred_element_type=f32
            )
            scores = jnp.where(seen, scores * scale_factor, -1e30)
            expo = jnp.exp(scores - jnp.max(scores, axis=1, keepdims=True))
            weight = (expo / jnp.sum(expo, axis=1, keepdims=True)).astype(bf16)
            result = jnp.dot(weight, values, preferred_element_type=f32)
            for token in range(pair):
                attended_buf[far, pl.ds(first + token, group_size, stride=block), :] = result[
                    token * group_size : (token + 1) * group_size
                ]
    for far in range(head_devices):
        for at in range(group_size):
            attended_send[far, :, at * head_dim : (at + 1) * head_dim] = attended_buf[
                far, at * block : (at + 1) * block, :
            ].astype(bf16)

    def att_hop(off):
        other, place_of = member(off)
        return hop(
            attended_send.at[place_of["gy"]],
            attended_recv.at[source_at],
            att_sends.at[other],
            att_recvs.at[mine],
            place_of,
        )

    def source_of(other, which):
        return ((other // head_devices) * 2 + which) * head_devices + lax.rem(other, head_devices)

    def att_arrival(off):
        other, place_of = member(off)
        return hop(
            attended_send.at[place_of["gy"]],
            attended_recv.at[source_of(other, core)],
            att_sends.at[other],
            att_recvs.at[other],
            place_of,
        )

    def pair_hop(other, which):
        from_at = source_of(other, which)
        return hop(
            attended_recv.at[from_at],
            attended_recv.at[from_at],
            pair_sends.at[other],
            pair_recvs.at[other],
            partner,
        )

    for off in range(team - 1, 0, -1):
        att_hop(off).start()
    attended_recv[source_at] = attended_send[head]
    pair_hop(mine, core).start()
    for off in range(1, team):
        att_arrival(off).wait_recv()
        pair_hop(lax.rem(mine + off, team), core).start()
    for off in range(team):
        pair_hop(lax.rem(mine + off, team), 1 - core).wait_recv()

    heads_width = group_size * head_dim
    sources = places * head_devices
    first_rows = lax.rem(lax.broadcasted_iota(jnp.int32, (2 * block, heads_width), 0), block) // near
    for at in range(0, sources, 2):
        both = jnp.concatenate([attended_recv[at], attended_recv[at + 1]], axis=0).astype(f32)
        for group in range(groups):
            left[at * block : (at + 2) * block, group * heads_width : (group + 1) * heads_width] = (
                jnp.where(first_rows == group, both, 0.0).astype(bf16)
            )

    def part_hop(at, off):
        other = lax.rem(head + off, head_devices)
        return hop(
            part_send.at[at, other],
            part_recv.at[at, head],
            part_sends.at[at, other],
            part_recvs.at[at, head],
            {"gy": other},
        )

    def part_arrival(at, off):
        other = lax.rem(head + off, head_devices)
        return hop(
            part_send.at[at, other],
            part_recv.at[at, other],
            part_sends.at[at, other],
            part_recvs.at[at, other],
            {"gy": other},
        )

    across = part_own.shape[2]
    share = total_tokens // head_devices

    @pl.loop(0, stretches)
    def _(at):
        weight_copy(at).wait()
        span = pl.ds(pl.multiple_of(at * across, across), across)
        product = jnp.dot(
            left[:, : groups * heads_width], weights[:, span], preferred_element_type=f32
        )
        upper = lax.broadcasted_iota(jnp.int32, (block, across), 0) < near
        tiles = []
        for source in range(sources):
            tile = product[source * block : (source + 1) * block]
            tiles.append(tile + pltpu.roll(tile, near, 0))
        joined = [
            jnp.where(upper, tiles[source], tiles[source + 1]) for source in range(0, sources, 2)
        ]
        per = len(joined) // head_devices
        for far in range(head_devices):
            value = jnp.concatenate(joined[far * per : (far + 1) * per], axis=0)
            part_send[at, far] = value.astype(bf16)

            @pl.when(far == head)
            def _():
                part_own[at] = value

        for off in range(1, head_devices):
            part_hop(at, off).start()

    mine_rows = pl.ds(pl.multiple_of(head * share, share), share)

    @pl.loop(0, stretches)
    def _(at):
        span = pl.ds(pl.multiple_of(at * across, across), across)
        value = part_own[at] + tok[mine_rows, span].astype(f32)
        for off in range(1, head_devices):
            part_arrival(at, off).wait_recv()
            value = value + part_recv[at, lax.rem(head + off, head_devices)].astype(f32)
        out_ref[:, span] = value

    square_hop.wait_send()
    for off in range(1, lanes):
        square_send(off).wait_send()

    @pl.loop(0, pieces)
    def _(piece):
        core_hop(piece).wait_send()
        for off in range(1, team):
            row_hop(piece, off).wait_send()

    for off in range(1, team):
        att_hop(off).wait_send()
    for off in range(team):
        pair_hop(lax.rem(mine + off, team), core).wait_send()

    @pl.loop(0, stretches)
    def _(at):
        for off in range(1, head_devices):
            part_hop(at, off).wait_send()


def whole_block(tokens, norm_gain, qkv_weight, out_weight, kv_cache, lengths, positions):
    f32, bf16 = jnp.float32, jnp.bfloat16
    rows_total, pair, local_width = tokens.shape
    groups, columns, head_dim = qkv_weight.shape[1:]
    places, head_devices = lax.axis_size("gx"), lax.axis_size("gy")
    rows_local, max_len = kv_cache.shape[:2]
    total_tokens = rows_total * pair
    group_size = columns - 2
    pieces = columns // 2
    slots = 3
    lanes = places // 2
    team = lanes * head_devices
    block = groups * rows_local * pair
    sources = places * head_devices
    share = total_tokens // head_devices
    across = 512
    stretches = local_width // across
    contraction = local_width * groups
    wide = 2 * head_dim
    hbm = pl.BlockSpec(memory_space=pl.ANY)
    smem = pl.BlockSpec(memory_space=pltpu.SMEM)
    dma = pltpu.SemaphoreType.DMA
    got = pl.pallas_call(
        functools.partial(block_kernel, head_devices, places),
        out_shape=jax.ShapeDtypeStruct((share, local_width), f32),
        in_specs=[hbm, hbm, hbm, hbm, hbm, smem, smem],
        out_specs=pl.BlockSpec(memory_space=pltpu.VMEM),
        scratch_shapes=[
            pltpu.VMEM((rows_total, pair, local_width), bf16),
            pltpu.VMEM((total_tokens, local_width), bf16),
            pltpu.VMEM((local_width // 128, 128), bf16),
            pltpu.VMEM((local_width // 128, 128), f32),
            pltpu.VMEM((total_tokens * groups, contraction), bf16),
            pltpu.VMEM((slots, 2, local_width, groups, head_dim), bf16),
            pltpu.VMEM((2, 2 * contraction, head_dim), bf16),
            pltpu.VMEM((out_weight.shape[0] * head_dim, local_width), bf16),
            pltpu.VMEM((2, 2, team * block, wide), f32),
            pltpu.VMEM((pieces, team * block, wide), bf16),
            pltpu.VMEM((pieces, team * block, wide), bf16),
            pltpu.VMEM((pieces, team, block, wide), bf16),
            pltpu.VMEM((pieces, team, block, wide), bf16),
            pltpu.VMEM((2, team * block, 128), f32),
            pltpu.VMEM((team * block, 128), f32),
            pltpu.VMEM((team, block, 128), f32),
            pltpu.VMEM((lanes, block, 128), f32),
            pltpu.VMEM((head_devices, group_size * block, head_dim), f32),
            pltpu.VMEM((head_devices, group_size * block, head_dim), f32),
            pltpu.VMEM((head_devices, block, group_size * head_dim), bf16),
            pltpu.VMEM((sources, block, group_size * head_dim), bf16),
            pltpu.VMEM((stretches, head_devices, share, across), bf16),
            pltpu.VMEM((stretches, head_devices, share, across), bf16),
            pltpu.VMEM((stretches, share, across), f32),
            dma((4,)),
            dma((slots, 2)),
            dma((2,)),
            dma((stretches,)),
            dma((2, pieces)),
            dma((pieces, team)),
            dma((pieces, team)),
            dma((2 + 2 * lanes,)),
            dma((team,)),
            dma((team,)),
            dma((team,)),
            dma((team,)),
            dma((stretches, head_devices)),
            dma((stretches, head_devices)),
        ],
        compiler_params=pltpu.CompilerParams(
            collective_id=0, has_side_effects=True, vmem_limit_bytes=63 << 20
        ),
    )(
        tokens,
        norm_gain.reshape(-1, 128),
        jnp.transpose(qkv_weight, (0, 2, 1, 3)),
        out_weight.reshape(-1, local_width),
        kv_cache.reshape(-1, head_dim),
        lengths,
        positions,
    )
    return got.reshape(share // pair, pair, local_width)


def body(tokens, norm_gain, qkv_weight, out_weight, kv_cache, lengths, positions):
    rows_local = kv_cache.shape[0]
    head_devices = lax.axis_size("gy")
    width_index = lax.axis_index("gx")
    head_index = lax.axis_index("gy")
    total_rows = tokens.shape[0]
    local_width = tokens.shape[2]
    groups_local = qkv_weight.shape[1]
    group_width = qkv_weight.shape[2]
    head_dim = qkv_weight.shape[3]
    group_size = group_width - 2
    block_rows = rows_local * head_devices
    places = lax.axis_size("gx")
    pair = tokens.shape[1]
    contraction = local_width * groups_local
    resident = (
        out_weight.size
        + 10 * contraction * head_dim
        + total_rows * pair * (2 * local_width + groups_local * contraction)
    )
    if (
        groups_local * rows_local * pair == 8
        and places % 2 == 0
        and head_devices > 1
        and total_rows == rows_local * places * head_devices
        and places % head_devices == 0
        and group_width % 2 == 0
        and head_dim == 128
        and kv_cache.shape[1] % 32 == 0
        and local_width % 512 == 0
        and 2 * resident < 59 << 20
    ):
        return whole_block(
            tokens, norm_gain, qkv_weight, out_weight, kv_cache, lengths, positions
        )
    tokens_wide = tokens.astype(jnp.float32)
    hidden = (tokens_wide * norm_gain.astype(jnp.float32)).astype(jnp.bfloat16)
    squares = jnp.sum(tokens_wide * tokens_wide, axis=-1)
    partial_value = jnp.dot(
        hidden.reshape(total_rows * 2, local_width),
        qkv_weight.reshape(local_width, -1),
        preferred_element_type=jnp.float32,
    )
    partial_value = partial_value.reshape(total_rows, 2, groups_local, group_width, head_dim)
    block_sum, block_squares = (
        lax.psum_scatter(partial_value, "gx", scatter_dimension=0, tiled=True),
        lax.psum_scatter(squares, "gx", scatter_dimension=0, tiled=True),
    )
    inv_rms = lax.rsqrt(block_squares / D + norm_eps)
    ready = finish(
        block_sum * inv_rms[:, :, None, None, None], positions, width_index * block_rows, block_rows
    )
    packed = lax.all_to_all(ready, "gy", split_axis=0, concat_axis=2, tiled=True)
    queries = packed[:, :, :, :group_size]
    key_new = packed[:, :, :, group_size]
    value_new = packed[:, :, :, group_size + 1]
    attended = attend(queries, key_new, value_new, kv_cache, lengths)
    regrouped = lax.all_to_all(attended, "gy", split_axis=2, concat_axis=0, tiled=True)
    out_flat = out_weight.reshape(-1, local_width)
    row_piece = lax.all_gather(regrouped, "gx", axis=0, tiled=True)
    piece_rows = row_piece.shape[0]
    product = jnp.dot(
        row_piece.reshape(piece_rows * 2, -1), out_flat, preferred_element_type=jnp.float32
    )
    terms = product.astype(jnp.bfloat16).reshape(head_devices, -1, 2, local_width)
    arrived = lax.all_to_all(terms, "gy", split_axis=0, concat_axis=0)
    own_sum = jnp.sum(arrived.astype(jnp.float32), axis=0)
    row_share = total_rows // head_devices
    residual = lax.dynamic_slice_in_dim(tokens, head_index * row_share, row_share, 0).astype(
        jnp.float32
    )
    return residual + own_sum


def solution(mesh):
    return jax.shard_map(
        body,
        mesh=mesh,
        in_specs=(
            P("groups", None, "gx"),
            P("gx"),
            P("gx", "gy", None, None),
            P("gy", None, "gx"),
            P(("groups", "gx", "gy"), None, None, None, None),
            P(("groups", "gx", "gy")),
            P("groups"),
        ),
        out_specs=P(("groups", "gy"), None, "gx"),
        check_vma=False,
    )
```

```python
import functools
import itertools
import math

import jax
import jax.numpy as jnp
from jax import lax
from jax.experimental import pallas as pl
from jax.experimental.pallas import tpu as pltpu
from jax.sharding import PartitionSpec as P

D = 16384


norm_eps = 1e-05
rope_base = 500000.0


def rotate(values, places):
    half_dim = values.shape[-1] // 2
    index_half = jnp.arange(half_dim, dtype=jnp.float32)
    frequency = rope_base ** (-2.0 * index_half / values.shape[-1])
    angles = places[..., None] * frequency
    cosine = jnp.cos(angles)
    sine_part = jnp.sin(angles)
    front_half = values[..., :half_dim]
    back_half = values[..., half_dim:]
    return jnp.concatenate(
        [front_half * cosine - back_half * sine_part, back_half * cosine + front_half * sine_part],
        axis=-1,
    )


def finish(projected, positions, first_row, row_count):
    group_size = projected.shape[3] - 2
    placed = lax.dynamic_slice_in_dim(positions, first_row, row_count, 0)
    places = (placed[:, None] + jnp.arange(2, dtype=jnp.int32)[None, :]).astype(jnp.float32)
    queries = rotate(projected[:, :, :, :group_size], places[:, :, None, None])
    key_new = rotate(projected[:, :, :, group_size : group_size + 1], places[:, :, None, None])
    value_new = projected[:, :, :, group_size + 1 :]
    return jnp.concatenate([queries, key_new, value_new], axis=3).astype(jnp.bfloat16)


def attend(queries, key_new, value_new, cache_rows, length):
    scale_factor = 1.0 / math.sqrt(queries.shape[-1])
    scores_old = (
        jnp.einsum(
            "rtgid,rsgd->rtgis", queries, cache_rows[:, :, 0], preferred_element_type=jnp.float32
        )
        * scale_factor
    )
    slot_ids = jnp.arange(cache_rows.shape[1], dtype=jnp.int32)
    visible = slot_ids[None, :] < length[:, None]
    scores_old = jnp.where(visible[:, None, None, None, :], scores_old, -1e30)
    scores_new = (
        jnp.einsum("rtgid,rugd->rtgiu", queries, key_new, preferred_element_type=jnp.float32)
        * scale_factor
    )
    token_ids = jnp.arange(queries.shape[1], dtype=jnp.int32)
    causal = token_ids[:, None] >= token_ids[None, :]
    scores_new = jnp.where(causal[None, :, None, None, :], scores_new, -1e30)
    highest = jnp.maximum(jnp.max(scores_old, axis=-1), jnp.max(scores_new, axis=-1))
    expo_old = jnp.exp(scores_old - highest[..., None])
    expo_new = jnp.exp(scores_new - highest[..., None])
    denominator = jnp.sum(expo_old, axis=-1) + jnp.sum(expo_new, axis=-1)
    weight_old = (expo_old / denominator[..., None]).astype(jnp.bfloat16)
    weight_new = (expo_new / denominator[..., None]).astype(jnp.bfloat16)
    attended = jnp.einsum(
        "rtgis,rsgd->rtgid", weight_old, cache_rows[:, :, 1], preferred_element_type=jnp.float32
    )
    attended = attended + jnp.einsum(
        "rtgiu,rugd->rtgid", weight_new, value_new, preferred_element_type=jnp.float32
    )
    return attended.astype(jnp.bfloat16)


def hop(source, target, sends, arrivals, place):
    return pltpu.make_async_remote_copy(
        src_ref=source,
        dst_ref=target,
        send_sem=sends,
        recv_sem=arrivals,
        device_id=place,
        device_id_type=pl.DeviceIdType.MESH,
    )


def block_kernel(
    head_devices,
    places,
    tokens_ref,
    gain_ref,
    qkv_ref,
    out_weight_ref,
    cache_ref,
    lengths_ref,
    positions_ref,
    out_ref,
    tok,
    gain,
    gain_wide,
    left,
    ring,
    chunk,
    weights,
    own_sum,
    core_send,
    core_recv,
    row_send,
    row_recv,
    square_all,
    square_core,
    square_mid,
    square_recv,
    query_buf,
    attended_buf,
    attended_send,
    attended_recv,
    part_send,
    part_recv,
    part_own,
    load_sems,
    ring_sems,
    tile_sems,
    weight_sems,
    core_sems,
    row_sends,
    row_recvs,
    square_sems,
    att_sends,
    att_recvs,
    pair_sends,
    pair_recvs,
    part_sends,
    part_recvs,
):
    f32, bf16 = jnp.float32, jnp.bfloat16
    rows_total, pair, local_width = tokens_ref.shape
    total_tokens = rows_total * pair
    columns, head_dim = qkv_ref.shape[1], qkv_ref.shape[3]
    groups = qkv_ref.shape[2]
    group_size = columns - 2
    pieces = columns // 2
    slots = ring.shape[0]
    max_len = (cache_ref.shape[0] // (2 * groups * head_devices)) // lengths_ref.shape[0]
    rows_local = lengths_ref.shape[0]
    all_groups = groups * head_devices
    near = rows_local * pair
    block = groups * near
    lanes = places // 2
    team = lanes * head_devices
    contraction = local_width * groups
    width = lax.axis_index("gx")
    head = lax.axis_index("gy")
    core = lax.rem(width, 2)
    lane_at = width // 2
    mine = lane_at * head_devices + head
    source_at = width * head_devices + head
    partner = {"gx": width + 1 - 2 * core}

    def member(off):
        other = lax.rem(mine + off, team)
        far_lane, far_head = other // head_devices, lax.rem(other, head_devices)
        return other, {"gx": far_lane * 2 + core, "gy": far_head}

    def bring(piece, slot):
        return [
            pltpu.make_async_copy(
                qkv_ref.at[:, piece * 2 + at], ring.at[slot, at], ring_sems.at[slot, at]
            )
            for at in range(2)
        ]

    load_tokens = pltpu.make_async_copy(
        tokens_ref.reshape(total_tokens, local_width), tok, load_sems.at[0]
    )
    load_gain = pltpu.make_async_copy(gain_ref, gain, load_sems.at[1])
    load_tokens.start()
    load_gain.start()
    for piece in range(min(slots, pieces)):
        for copy in bring(piece, piece):
            copy.start()
    barrier = pltpu.get_barrier_semaphore()
    pl.semaphore_signal(barrier, inc=1, device_id=partner, device_id_type=pl.DeviceIdType.MESH)
    for off in range(1, team):
        pl.semaphore_signal(
            barrier, inc=1, device_id=member(off)[1], device_id_type=pl.DeviceIdType.MESH
        )

    made = lax.broadcasted_iota(jnp.int32, (total_tokens * groups, total_tokens), 0)
    held = lax.broadcasted_iota(jnp.int32, (total_tokens * groups, total_tokens), 1)
    target = made // block
    owner_core = target // team
    owner_lane = lax.rem(target, team) // head_devices
    owner_head = lax.rem(target, head_devices)
    owner = (owner_lane * 2 + owner_core) * head_devices + owner_head
    chosen = owner * near + lax.rem(made, near) == held
    chooser = jnp.where(chosen, 1.0, 0.0)
    group_row = lax.rem(
        lax.broadcasted_iota(jnp.int32, (total_tokens * groups, 128), 0), block
    ) // near
    feature = lax.broadcasted_iota(jnp.int32, (128 * groups, 128 * groups), 0)
    goal = lax.broadcasted_iota(jnp.int32, (128 * groups, 128 * groups), 1)
    spread = jnp.where(
        goal == lax.rem(feature, 128) * groups + feature // 128, 1.0, 0.0
    ).astype(bf16)

    load_tokens.wait()
    load_gain.wait()
    gain_wide[...] = gain[...].astype(f32)
    depth = 1024

    def widen(at, squares):
        start = pl.multiple_of(at * depth, depth)
        wide = tok[:, pl.ds(start, depth)].astype(f32)
        scale = jnp.concatenate(
            [gain_wide[pl.ds(at * (depth // 128) + q, 1), :] for q in range(depth // 128)], axis=1
        )
        hidden = (wide * scale).astype(bf16)
        ordered = jnp.dot(chooser.astype(bf16), hidden, preferred_element_type=f32)
        for q in range(depth // 128):
            part = wide[:, q * 128 : (q + 1) * 128]
            squares += part * part
            near_part = ordered[:, q * 128 : (q + 1) * 128]
            split = jnp.concatenate(
                [jnp.where(group_row == group, near_part, 0.0) for group in range(groups)], axis=1
            ).astype(bf16)
            begin = pl.multiple_of((start + q * 128) * groups, 128 * groups)
            left[:, pl.ds(begin, 128 * groups)] = jnp.dot(
                split, spread, preferred_element_type=f32
            ).astype(bf16)
        return squares

    squares = lax.fori_loop(
        0, local_width // depth, widen, jnp.zeros((total_tokens, 128), f32)
    )
    square_all[...] = jnp.dot(
        chooser, squares, preferred_element_type=f32, precision=lax.Precision.HIGHEST
    ).reshape(square_all.shape)
    pl.semaphore_wait(barrier, team)

    square_hop = hop(
        square_all.at[1 - core], square_core, square_sems.at[0], square_sems.at[1], partner
    )
    square_hop.start()

    def core_hop(piece):
        return hop(
            core_send.at[piece],
            core_recv.at[piece],
            core_sems.at[0, piece],
            core_sems.at[1, piece],
            partner,
        )

    def row_hop(piece, off):
        other, place = member(off)
        return hop(
            row_send.at[piece, other],
            row_recv.at[piece, mine],
            row_sends.at[piece, other],
            row_recvs.at[piece, mine],
            place,
        )

    def row_arrival(piece, off):
        other, place = member(off)
        return hop(
            row_send.at[piece, other],
            row_recv.at[piece, other],
            row_sends.at[piece, other],
            row_recvs.at[piece, other],
            place,
        )

    def pass_on(piece):
        core_hop(piece).wait_recv()
        total = own_sum[lax.rem(piece, 2), core] + core_recv[piece].astype(f32)
        row_send[piece] = total.reshape(row_send.shape[1:]).astype(bf16)
        row_recv[piece, mine] = row_send[piece, mine]
        for off in range(1, team):
            row_hop(piece, off).start()

    def weight_copy(at):
        across = part_own.shape[2]
        return pltpu.make_async_copy(
            out_weight_ref.at[:, pl.ds(at * across, across)],
            weights.at[:, pl.ds(at * across, across)],
            weight_sems.at[at],
        )

    stretches = part_own.shape[0]
    cache_slot, cached_slot = pieces % 2, (pieces - 1) % 2
    cache_rows = cache_ref.shape[0]
    load_cache = pltpu.make_async_copy(
        cache_ref, chunk.at[cache_slot, pl.ds(0, cache_rows)], load_sems.at[3]
    )

    @pl.loop(0, pieces)
    def _(piece):
        slot, here = lax.rem(piece, slots), lax.rem(piece, 2)
        for copy in bring(piece, slot):
            copy.wait()
        flat = ring.reshape(slots, 2, contraction, head_dim)
        moves = [
            pltpu.make_async_copy(
                flat.at[slot, at],
                chunk.at[here, pl.ds(at * contraction, contraction)],
                tile_sems.at[at],
            )
            for at in range(2)
        ]
        for move in moves:
            move.start()

        @pl.when(piece == pieces - 1)
        def _():
            load_cache.start()

        for move in moves:
            move.wait()

        @pl.when(piece + slots < pieces)
        def _():
            for copy in bring(piece + slots, slot):
                copy.start()

        right = jnp.concatenate(
            [chunk[here, pl.ds(0, contraction)], chunk[here, pl.ds(contraction, contraction)]], axis=1
        )
        total = jnp.dot(left[...], right, preferred_element_type=f32)
        own_sum[here] = total.reshape(own_sum.shape[1:])
        core_send[piece] = own_sum[here, 1 - core].astype(bf16)
        core_hop(piece).start()

        @pl.when(piece >= 1)
        def _():
            pass_on(piece - 1)

    pass_on(pieces - 1)
    square_hop.wait_recv()
    square_mid[...] = (square_all[core] + square_core[...]).reshape(square_mid.shape)
    square_recv[lane_at] = square_mid[mine]

    def square_send(off):
        other_lane = lax.rem(lane_at + off, lanes)
        return hop(
            square_mid.at[other_lane * head_devices + head],
            square_recv.at[lane_at],
            square_sems.at[2 + 2 * off],
            square_sems.at[3 + 2 * off],
            {"gx": other_lane * 2 + core},
        )

    def square_arrival(off):
        other_lane = lax.rem(lane_at + lanes - off, lanes)
        return hop(
            square_mid.at[mine],
            square_recv.at[other_lane],
            square_sems.at[2 + 2 * off],
            square_sems.at[3 + 2 * off],
            {"gx": other_lane * 2 + core},
        )

    for off in range(1, lanes):
        square_send(off).start()
    early = stretches // 2
    for at in range(early):
        weight_copy(at).start()

    stride = max_len + 16
    steps = 16
    kinds = 2 * all_groups
    size = steps * kinds
    to_row = lax.broadcasted_iota(jnp.int32, (size, size), 0)
    from_row = lax.broadcasted_iota(jnp.int32, (size, size), 1)
    regroup = jnp.where(
        from_row == lax.rem(to_row, steps) * kinds + to_row // steps, 1.0, 0.0
    ).astype(bf16)
    load_cache.wait()
    for row in range(rows_local):

        @pl.loop(0, max_len // (2 * steps))
        def _(step):
            first = pl.multiple_of(row * max_len * kinds + step * 2 * size, size)
            both = jnp.concatenate(
                [chunk[cache_slot, pl.ds(first, size)], chunk[cache_slot, pl.ds(first + size, size)]],
                axis=1,
            )
            sorted_rows = jnp.dot(regroup, both, preferred_element_type=f32).astype(bf16)
            for kind in range(kinds):
                base = (row * kinds + kind) * stride
                for half in range(2):
                    at = pl.multiple_of(base + (step * 2 + half) * steps, 16)
                    chunk[cached_slot, pl.ds(at, steps)] = sorted_rows[
                        kind * steps : (kind + 1) * steps, half * head_dim : (half + 1) * head_dim
                    ]

    row_at = lax.broadcasted_iota(jnp.int32, (block, head_dim), 0)
    lane = lax.broadcasted_iota(jnp.int32, (block, head_dim), 1)
    half_dim = head_dim // 2
    place = jnp.zeros((block, head_dim), jnp.int32)
    for row in range(rows_local):
        place = jnp.where(
            lax.rem(row_at, near) // pair == row, positions_ref[source_at * rows_local + row], place
        )
    place = (place + lax.rem(row_at, pair)).astype(f32)
    index_half = lax.rem(lane, half_dim).astype(f32)
    frequency = jnp.exp(index_half * (-2.0 * math.log(rope_base) / head_dim))
    angles = place * frequency
    cosine = jnp.cos(angles)
    sine = jnp.where(lane < half_dim, -jnp.sin(angles), jnp.sin(angles))

    for off in range(1, lanes):
        square_arrival(off).wait_recv()
    square_total = square_recv[0]
    for at in range(1, lanes):
        square_total = square_total + square_recv[at]
    inv_rms = lax.rsqrt(
        jnp.sum(square_total, axis=1, keepdims=True) / (local_width * places) + norm_eps
    )

    @pl.loop(0, pieces)
    def _(piece):
        for off in range(1, team):
            row_arrival(piece, off).wait_recv()

    small = lax.broadcasted_iota(jnp.int32, (block, head_dim), 0)
    for far in range(head_devices):
        for column in range(columns):
            piece, side = column // 2, column % 2
            value = row_recv[piece, far, :, side * head_dim : (side + 1) * head_dim].astype(f32)
            for at in range(1, lanes):
                value = value + row_recv[
                    piece, at * head_devices + far, :, side * head_dim : (side + 1) * head_dim
                ].astype(f32)
            value = value * inv_rms
            if column <= group_size:
                turned = jnp.concatenate([value[:, half_dim:], value[:, :half_dim]], axis=1)
                value = value * cosine + turned * sine
            if column < group_size:
                query_buf[far, column * block : (column + 1) * block, :] = value
            else:
                kind = column - group_size
                for group in range(groups):
                    for row in range(rows_local):
                        start = group * near + row * pair
                        moved = pltpu.roll(value, (block - start) % block, 0) if start else value
                        fresh = jnp.where(small < pair, moved, 0.0)
                        base = (
                            row * kinds + kind * all_groups + far * groups + group
                        ) * stride + max_len
                        chunk[cached_slot, pl.ds(base, 16)] = jnp.concatenate(
                            [fresh, jnp.zeros((16 - block, head_dim), f32)], axis=0
                        ).astype(bf16)

    scale_factor = 1.0 / math.sqrt(head_dim)
    count = pair * group_size
    slot_id = lax.broadcasted_iota(jnp.int32, (count, stride), 1)
    token_id = lax.broadcasted_iota(jnp.int32, (count, stride), 0) // group_size
    fresh_seen = (slot_id >= max_len) & (slot_id - max_len <= token_id)
    for row in range(rows_local):
        seen = (slot_id < lengths_ref[row]) | fresh_seen
        for every in range(all_groups):
            far, group = every // groups, every % groups
            first = group * near + row * pair
            queries = jnp.concatenate(
                [
                    query_buf[far, pl.ds(first + token, group_size, stride=block), :]
                    for token in range(pair)
                ],
                axis=0,
            ).astype(bf16)
            keys = chunk[cached_slot, pl.ds((row * kinds + every) * stride, stride)]
            values = chunk[cached_slot, pl.ds((row * kinds + all_groups + every) * stride, stride)]
            scores = lax.dot_general(
                queries, keys, (((1,), (1,)), ((), ())), preferred_element_type=f32
            )
            scores = jnp.where(seen, scores * scale_factor, -1e30)
            expo = jnp.exp(scores - jnp.max(scores, axis=1, keepdims=True))
            weight = (expo / jnp.sum(expo, axis=1, keepdims=True)).astype(bf16)
            result = jnp.dot(weight, values, preferred_element_type=f32)
            for token in range(pair):
                attended_buf[far, pl.ds(first + token, group_size, stride=block), :] = result[
                    token * group_size : (token + 1) * group_size
                ]
    for far in range(head_devices):
        for at in range(group_size):
            attended_send[far, :, at * head_dim : (at + 1) * head_dim] = attended_buf[
                far, at * block : (at + 1) * block, :
            ].astype(bf16)

    def att_hop(off):
        other, place_of = member(off)
        return hop(
            attended_send.at[place_of["gy"]],
            attended_recv.at[source_at],
            att_sends.at[other],
            att_recvs.at[mine],
            place_of,
        )

    def source_of(other, which):
        return ((other // head_devices) * 2 + which) * head_devices + lax.rem(other, head_devices)

    def att_arrival(off):
        other, place_of = member(off)
        return hop(
            attended_send.at[place_of["gy"]],
            attended_recv.at[source_of(other, core)],
            att_sends.at[other],
            att_recvs.at[other],
            place_of,
        )

    def pair_hop(other, which):
        from_at = source_of(other, which)
        return hop(
            attended_recv.at[from_at],
            attended_recv.at[from_at],
            pair_sends.at[other],
            pair_recvs.at[other],
            partner,
        )

    for off in range(team - 1, 0, -1):
        att_hop(off).start()
    attended_recv[source_at] = attended_send[head]
    pair_hop(mine, core).start()
    later = iter(range(early, stretches))
    for off in range(1, team):
        for at in itertools.islice(later, 2):
            weight_copy(at).start()
        att_arrival(off).wait_recv()
        pair_hop(lax.rem(mine + off, team), core).start()
    for at in later:
        weight_copy(at).start()
    for off in range(team):
        pair_hop(lax.rem(mine + off, team), 1 - core).wait_recv()

    heads_width = group_size * head_dim
    sources = places * head_devices
    first_rows = lax.rem(lax.broadcasted_iota(jnp.int32, (2 * block, heads_width), 0), block) // near
    for at in range(0, sources, 2):
        both = jnp.concatenate([attended_recv[at], attended_recv[at + 1]], axis=0).astype(f32)
        for group in range(groups):
            left[at * block : (at + 2) * block, group * heads_width : (group + 1) * heads_width] = (
                jnp.where(first_rows == group, both, 0.0).astype(bf16)
            )

    def part_hop(at, off):
        other = lax.rem(head + off, head_devices)
        return hop(
            part_send.at[at, other],
            part_recv.at[at, head],
            part_sends.at[at, other],
            part_recvs.at[at, head],
            {"gy": other},
        )

    def part_arrival(at, off):
        other = lax.rem(head + off, head_devices)
        return hop(
            part_send.at[at, other],
            part_recv.at[at, other],
            part_sends.at[at, other],
            part_recvs.at[at, other],
            {"gy": other},
        )

    across = part_own.shape[2]
    share = total_tokens // head_devices

    @pl.loop(0, stretches)
    def _(at):
        weight_copy(at).wait()
        span = pl.ds(pl.multiple_of(at * across, across), across)
        product = jnp.dot(
            left[:, : groups * heads_width], weights[:, span], preferred_element_type=f32
        )
        upper = lax.broadcasted_iota(jnp.int32, (block, across), 0) < near
        tiles = []
        for source in range(sources):
            tile = product[source * block : (source + 1) * block]
            tiles.append(tile + pltpu.roll(tile, near, 0))
        joined = [
            jnp.where(upper, tiles[source], tiles[source + 1]) for source in range(0, sources, 2)
        ]
        per = len(joined) // head_devices
        for far in range(head_devices):
            value = jnp.concatenate(joined[far * per : (far + 1) * per], axis=0)
            part_send[at, far] = value.astype(bf16)

            @pl.when(far == head)
            def _():
                part_own[at] = value

        for off in range(1, head_devices):
            part_hop(at, off).start()

    mine_rows = pl.ds(pl.multiple_of(head * share, share), share)

    @pl.loop(0, stretches)
    def _(at):
        span = pl.ds(pl.multiple_of(at * across, across), across)
        value = part_own[at] + tok[mine_rows, span].astype(f32)
        for off in range(1, head_devices):
            part_arrival(at, off).wait_recv()
            value = value + part_recv[at, lax.rem(head + off, head_devices)].astype(f32)
        out_ref[:, span] = value

    square_hop.wait_send()
    for off in range(1, lanes):
        square_send(off).wait_send()

    @pl.loop(0, pieces)
    def _(piece):
        core_hop(piece).wait_send()
        for off in range(1, team):
            row_hop(piece, off).wait_send()

    for off in range(1, team):
        att_hop(off).wait_send()
    for off in range(team):
        pair_hop(lax.rem(mine + off, team), core).wait_send()

    @pl.loop(0, stretches)
    def _(at):
        for off in range(1, head_devices):
            part_hop(at, off).wait_send()


def whole_block(tokens, norm_gain, qkv_weight, out_weight, kv_cache, lengths, positions):
    f32, bf16 = jnp.float32, jnp.bfloat16
    rows_total, pair, local_width = tokens.shape
    groups, columns, head_dim = qkv_weight.shape[1:]
    places, head_devices = lax.axis_size("gx"), lax.axis_size("gy")
    rows_local, max_len = kv_cache.shape[:2]
    total_tokens = rows_total * pair
    group_size = columns - 2
    pieces = columns // 2
    slots = 3
    lanes = places // 2
    team = lanes * head_devices
    block = groups * rows_local * pair
    sources = places * head_devices
    share = total_tokens // head_devices
    across = 512
    stretches = local_width // across
    contraction = local_width * groups
    wide = 2 * head_dim
    hbm = pl.BlockSpec(memory_space=pl.ANY)
    smem = pl.BlockSpec(memory_space=pltpu.SMEM)
    dma = pltpu.SemaphoreType.DMA
    got = pl.pallas_call(
        functools.partial(block_kernel, head_devices, places),
        out_shape=jax.ShapeDtypeStruct((share, local_width), f32),
        in_specs=[hbm, hbm, hbm, hbm, hbm, smem, smem],
        out_specs=pl.BlockSpec(memory_space=pltpu.VMEM),
        scratch_shapes=[
            pltpu.VMEM((total_tokens, local_width), bf16),
            pltpu.VMEM((local_width // 128, 128), bf16),
            pltpu.VMEM((local_width // 128, 128), f32),
            pltpu.VMEM((total_tokens * groups, contraction), bf16),
            pltpu.VMEM((slots, 2, local_width, groups, head_dim), bf16),
            pltpu.VMEM((2, 2 * contraction, head_dim), bf16),
            pltpu.VMEM((out_weight.shape[0] * head_dim, local_width), bf16),
            pltpu.VMEM((2, 2, team * block, wide), f32),
            pltpu.VMEM((pieces, team * block, wide), bf16),
            pltpu.VMEM((pieces, team * block, wide), bf16),
            pltpu.VMEM((pieces, team, block, wide), bf16),
            pltpu.VMEM((pieces, team, block, wide), bf16),
            pltpu.VMEM((2, team * block, 128), f32),
            pltpu.VMEM((team * block, 128), f32),
            pltpu.VMEM((team, block, 128), f32),
            pltpu.VMEM((lanes, block, 128), f32),
            pltpu.VMEM((head_devices, group_size * block, head_dim), f32),
            pltpu.VMEM((head_devices, group_size * block, head_dim), f32),
            pltpu.VMEM((head_devices, block, group_size * head_dim), bf16),
            pltpu.VMEM((sources, block, group_size * head_dim), bf16),
            pltpu.VMEM((stretches, head_devices, share, across), bf16),
            pltpu.VMEM((stretches, head_devices, share, across), bf16),
            pltpu.VMEM((stretches, share, across), f32),
            dma((4,)),
            dma((slots, 2)),
            dma((2,)),
            dma((stretches,)),
            dma((2, pieces)),
            dma((pieces, team)),
            dma((pieces, team)),
            dma((2 + 2 * lanes,)),
            dma((team,)),
            dma((team,)),
            dma((team,)),
            dma((team,)),
            dma((stretches, head_devices)),
            dma((stretches, head_devices)),
        ],
        compiler_params=pltpu.CompilerParams(
            collective_id=0, has_side_effects=True, vmem_limit_bytes=63 << 20
        ),
    )(
        tokens,
        norm_gain.reshape(-1, 128),
        jnp.transpose(qkv_weight, (0, 2, 1, 3)),
        out_weight.reshape(-1, local_width),
        kv_cache.reshape(-1, head_dim),
        lengths,
        positions,
    )
    return got.reshape(share // pair, pair, local_width)


def body(tokens, norm_gain, qkv_weight, out_weight, kv_cache, lengths, positions):
    rows_local = kv_cache.shape[0]
    head_devices = lax.axis_size("gy")
    width_index = lax.axis_index("gx")
    head_index = lax.axis_index("gy")
    total_rows = tokens.shape[0]
    local_width = tokens.shape[2]
    groups_local = qkv_weight.shape[1]
    group_width = qkv_weight.shape[2]
    head_dim = qkv_weight.shape[3]
    group_size = group_width - 2
    block_rows = rows_local * head_devices
    places = lax.axis_size("gx")
    pair = tokens.shape[1]
    contraction = local_width * groups_local
    resident = (
        out_weight.size
        + 10 * contraction * head_dim
        + total_rows * pair * (2 * local_width + groups_local * contraction)
    )
    if (
        groups_local * rows_local * pair == 8
        and places % 2 == 0
        and head_devices > 1
        and total_rows == rows_local * places * head_devices
        and places % head_devices == 0
        and group_width % 2 == 0
        and head_dim == 128
        and kv_cache.shape[1] % 32 == 0
        and local_width % 1024 == 0
        and 2 * resident < 59 << 20
    ):
        return whole_block(
            tokens, norm_gain, qkv_weight, out_weight, kv_cache, lengths, positions
        )
    tokens_wide = tokens.astype(jnp.float32)
    hidden = (tokens_wide * norm_gain.astype(jnp.float32)).astype(jnp.bfloat16)
    squares = jnp.sum(tokens_wide * tokens_wide, axis=-1)
    partial_value = jnp.dot(
        hidden.reshape(total_rows * 2, local_width),
        qkv_weight.reshape(local_width, -1),
        preferred_element_type=jnp.float32,
    )
    partial_value = partial_value.reshape(total_rows, 2, groups_local, group_width, head_dim)
    block_sum, block_squares = (
        lax.psum_scatter(partial_value, "gx", scatter_dimension=0, tiled=True),
        lax.psum_scatter(squares, "gx", scatter_dimension=0, tiled=True),
    )
    inv_rms = lax.rsqrt(block_squares / D + norm_eps)
    ready = finish(
        block_sum * inv_rms[:, :, None, None, None], positions, width_index * block_rows, block_rows
    )
    packed = lax.all_to_all(ready, "gy", split_axis=0, concat_axis=2, tiled=True)
    queries = packed[:, :, :, :group_size]
    key_new = packed[:, :, :, group_size]
    value_new = packed[:, :, :, group_size + 1]
    attended = attend(queries, key_new, value_new, kv_cache, lengths)
    regrouped = lax.all_to_all(attended, "gy", split_axis=2, concat_axis=0, tiled=True)
    out_flat = out_weight.reshape(-1, local_width)
    row_piece = lax.all_gather(regrouped, "gx", axis=0, tiled=True)
    piece_rows = row_piece.shape[0]
    product = jnp.dot(
        row_piece.reshape(piece_rows * 2, -1), out_flat, preferred_element_type=jnp.float32
    )
    terms = product.astype(jnp.bfloat16).reshape(head_devices, -1, 2, local_width)
    arrived = lax.all_to_all(terms, "gy", split_axis=0, concat_axis=0)
    own_sum = jnp.sum(arrived.astype(jnp.float32), axis=0)
    row_share = total_rows // head_devices
    residual = lax.dynamic_slice_in_dim(tokens, head_index * row_share, row_share, 0).astype(
        jnp.float32
    )
    return residual + own_sum


def solution(mesh):
    return jax.shard_map(
        body,
        mesh=mesh,
        in_specs=(
            P("groups", None, "gx"),
            P("gx"),
            P("gx", "gy", None, None),
            P("gy", None, "gx"),
            P(("groups", "gx", "gy"), None, None, None, None),
            P(("groups", "gx", "gy")),
            P("groups"),
        ),
        out_specs=P(("groups", "gy"), None, "gx"),
        check_vma=False,
    )
```

```python
import functools
import itertools
import math

import jax
import jax.numpy as jnp
from jax import lax
from jax.experimental import pallas as pl
from jax.experimental.pallas import tpu as pltpu
from jax.sharding import PartitionSpec as P

D = 16384


norm_eps = 1e-05
rope_base = 500000.0


def rotate(values, places):
    half_dim = values.shape[-1] // 2
    index_half = jnp.arange(half_dim, dtype=jnp.float32)
    frequency = rope_base ** (-2.0 * index_half / values.shape[-1])
    angles = places[..., None] * frequency
    cosine = jnp.cos(angles)
    sine_part = jnp.sin(angles)
    front_half = values[..., :half_dim]
    back_half = values[..., half_dim:]
    return jnp.concatenate(
        [front_half * cosine - back_half * sine_part, back_half * cosine + front_half * sine_part],
        axis=-1,
    )


def finish(projected, positions, first_row, row_count):
    group_size = projected.shape[3] - 2
    placed = lax.dynamic_slice_in_dim(positions, first_row, row_count, 0)
    places = (placed[:, None] + jnp.arange(2, dtype=jnp.int32)[None, :]).astype(jnp.float32)
    queries = rotate(projected[:, :, :, :group_size], places[:, :, None, None])
    key_new = rotate(projected[:, :, :, group_size : group_size + 1], places[:, :, None, None])
    value_new = projected[:, :, :, group_size + 1 :]
    return jnp.concatenate([queries, key_new, value_new], axis=3).astype(jnp.bfloat16)


def attend(queries, key_new, value_new, cache_rows, length):
    scale_factor = 1.0 / math.sqrt(queries.shape[-1])
    scores_old = (
        jnp.einsum(
            "rtgid,rsgd->rtgis", queries, cache_rows[:, :, 0], preferred_element_type=jnp.float32
        )
        * scale_factor
    )
    slot_ids = jnp.arange(cache_rows.shape[1], dtype=jnp.int32)
    visible = slot_ids[None, :] < length[:, None]
    scores_old = jnp.where(visible[:, None, None, None, :], scores_old, -1e30)
    scores_new = (
        jnp.einsum("rtgid,rugd->rtgiu", queries, key_new, preferred_element_type=jnp.float32)
        * scale_factor
    )
    token_ids = jnp.arange(queries.shape[1], dtype=jnp.int32)
    causal = token_ids[:, None] >= token_ids[None, :]
    scores_new = jnp.where(causal[None, :, None, None, :], scores_new, -1e30)
    highest = jnp.maximum(jnp.max(scores_old, axis=-1), jnp.max(scores_new, axis=-1))
    expo_old = jnp.exp(scores_old - highest[..., None])
    expo_new = jnp.exp(scores_new - highest[..., None])
    denominator = jnp.sum(expo_old, axis=-1) + jnp.sum(expo_new, axis=-1)
    weight_old = (expo_old / denominator[..., None]).astype(jnp.bfloat16)
    weight_new = (expo_new / denominator[..., None]).astype(jnp.bfloat16)
    attended = jnp.einsum(
        "rtgis,rsgd->rtgid", weight_old, cache_rows[:, :, 1], preferred_element_type=jnp.float32
    )
    attended = attended + jnp.einsum(
        "rtgiu,rugd->rtgid", weight_new, value_new, preferred_element_type=jnp.float32
    )
    return attended.astype(jnp.bfloat16)


def hop(source, target, sends, arrivals, place):
    return pltpu.make_async_remote_copy(
        src_ref=source,
        dst_ref=target,
        send_sem=sends,
        recv_sem=arrivals,
        device_id=place,
        device_id_type=pl.DeviceIdType.MESH,
    )


def block_kernel(
    head_devices,
    places,
    tokens_ref,
    gain_ref,
    qkv_ref,
    out_weight_ref,
    cache_ref,
    lengths_ref,
    positions_ref,
    out_ref,
    tok,
    gain,
    gain_wide,
    left,
    ring,
    chunk,
    weights,
    own_sum,
    core_send,
    core_recv,
    row_send,
    row_recv,
    square_all,
    square_core,
    square_mid,
    square_recv,
    query_buf,
    attended_buf,
    attended_send,
    attended_recv,
    part_send,
    part_recv,
    part_own,
    load_sems,
    ring_sems,
    tile_sems,
    weight_sems,
    core_sems,
    row_sends,
    row_recvs,
    square_sems,
    att_sends,
    att_recvs,
    pair_sends,
    pair_recvs,
    part_sends,
    part_recvs,
):
    f32, bf16 = jnp.float32, jnp.bfloat16
    rows_total, pair, local_width = tokens_ref.shape
    total_tokens = rows_total * pair
    columns, head_dim = qkv_ref.shape[1], qkv_ref.shape[3]
    groups = qkv_ref.shape[2]
    group_size = columns - 2
    pieces = columns // 2
    slots = ring.shape[0]
    max_len = (cache_ref.shape[0] // (2 * groups * head_devices)) // lengths_ref.shape[0]
    rows_local = lengths_ref.shape[0]
    all_groups = groups * head_devices
    near = rows_local * pair
    block = groups * near
    lanes = places // 2
    team = lanes * head_devices
    contraction = local_width * groups
    width = lax.axis_index("gx")
    head = lax.axis_index("gy")
    core = lax.rem(width, 2)
    lane_at = width // 2
    mine = lane_at * head_devices + head
    source_at = width * head_devices + head
    partner = {"gx": width + 1 - 2 * core}

    def member(off):
        other = lax.rem(mine + off, team)
        far_lane, far_head = other // head_devices, lax.rem(other, head_devices)
        return other, {"gx": far_lane * 2 + core, "gy": far_head}

    def bring(piece, slot):
        return [
            pltpu.make_async_copy(
                qkv_ref.at[:, piece * 2 + at], ring.at[slot, at], ring_sems.at[slot, at]
            )
            for at in range(2)
        ]

    load_tokens = pltpu.make_async_copy(
        tokens_ref.reshape(total_tokens, local_width), tok, load_sems.at[0]
    )
    load_gain = pltpu.make_async_copy(gain_ref, gain, load_sems.at[1])
    load_tokens.start()
    load_gain.start()
    for piece in range(min(slots, pieces)):
        for copy in bring(piece, piece):
            copy.start()
    barrier = pltpu.get_barrier_semaphore()
    pl.semaphore_signal(barrier, inc=1, device_id=partner, device_id_type=pl.DeviceIdType.MESH)
    for off in range(1, team):
        pl.semaphore_signal(
            barrier, inc=1, device_id=member(off)[1], device_id_type=pl.DeviceIdType.MESH
        )

    made = lax.broadcasted_iota(jnp.int32, (total_tokens * groups, total_tokens), 0)
    held = lax.broadcasted_iota(jnp.int32, (total_tokens * groups, total_tokens), 1)
    target = made // block
    owner_core = target // team
    owner_lane = lax.rem(target, team) // head_devices
    owner_head = lax.rem(target, head_devices)
    owner = (owner_lane * 2 + owner_core) * head_devices + owner_head
    chosen = owner * near + lax.rem(made, near) == held
    chooser = jnp.where(chosen, 1.0, 0.0)
    group_row = lax.rem(
        lax.broadcasted_iota(jnp.int32, (total_tokens * groups, 128), 0), block
    ) // near
    feature = lax.broadcasted_iota(jnp.int32, (128 * groups, 128 * groups), 0)
    goal = lax.broadcasted_iota(jnp.int32, (128 * groups, 128 * groups), 1)
    spread = jnp.where(
        goal == lax.rem(feature, 128) * groups + feature // 128, 1.0, 0.0
    ).astype(bf16)

    load_tokens.wait()
    load_gain.wait()
    gain_wide[...] = gain[...].astype(f32)
    depth = 1024

    def widen(at, squares):
        start = pl.multiple_of(at * depth, depth)
        wide = tok[:, pl.ds(start, depth)].astype(f32)
        scale = jnp.concatenate(
            [gain_wide[pl.ds(at * (depth // 128) + q, 1), :] for q in range(depth // 128)], axis=1
        )
        hidden = (wide * scale).astype(bf16)
        ordered = jnp.dot(chooser.astype(bf16), hidden, preferred_element_type=f32)
        for q in range(depth // 128):
            part = wide[:, q * 128 : (q + 1) * 128]
            squares += part * part
            near_part = ordered[:, q * 128 : (q + 1) * 128]
            split = jnp.concatenate(
                [jnp.where(group_row == group, near_part, 0.0) for group in range(groups)], axis=1
            ).astype(bf16)
            begin = pl.multiple_of((start + q * 128) * groups, 128 * groups)
            left[:, pl.ds(begin, 128 * groups)] = jnp.dot(
                split, spread, preferred_element_type=f32
            ).astype(bf16)
        return squares

    squares = lax.fori_loop(
        0, local_width // depth, widen, jnp.zeros((total_tokens, 128), f32)
    )
    square_all[...] = jnp.dot(
        chooser, squares, preferred_element_type=f32, precision=lax.Precision.HIGHEST
    ).reshape(square_all.shape)
    pl.semaphore_wait(barrier, team)

    square_hop = hop(
        square_all.at[1 - core], square_core, square_sems.at[0], square_sems.at[1], partner
    )
    square_hop.start()

    def core_hop(piece):
        return hop(
            core_send.at[piece],
            core_recv.at[piece],
            core_sems.at[0, piece],
            core_sems.at[1, piece],
            partner,
        )

    def row_hop(piece, off):
        other, place = member(off)
        return hop(
            row_send.at[piece, other],
            row_recv.at[piece, mine],
            row_sends.at[piece, other],
            row_recvs.at[piece, mine],
            place,
        )

    def row_arrival(piece, off):
        other, place = member(off)
        return hop(
            row_send.at[piece, other],
            row_recv.at[piece, other],
            row_sends.at[piece, other],
            row_recvs.at[piece, other],
            place,
        )

    def pass_on(piece):
        core_hop(piece).wait_recv()
        total = own_sum[lax.rem(piece, 3), core] + core_recv[piece].astype(f32)
        row_send[piece] = total.reshape(row_send.shape[1:]).astype(bf16)
        row_recv[piece, mine] = row_send[piece, mine]
        for off in range(1, team):
            row_hop(piece, off).start()

    def weight_copy(at):
        across = part_own.shape[2]
        return pltpu.make_async_copy(
            out_weight_ref.at[:, pl.ds(at * across, across)],
            weights.at[:, pl.ds(at * across, across)],
            weight_sems.at[at],
        )

    stretches = part_own.shape[0]
    cache_slot, cached_slot = pieces % 2, (pieces - 1) % 2
    cache_rows = cache_ref.shape[0]
    load_cache = pltpu.make_async_copy(
        cache_ref, chunk.at[cache_slot, pl.ds(0, cache_rows)], load_sems.at[3]
    )

    @pl.loop(0, pieces)
    def _(piece):
        slot, here = lax.rem(piece, slots), lax.rem(piece, 2)

        @pl.when(piece == pieces - 1)
        def _():
            load_cache.start()

        for copy in bring(piece, slot):
            copy.wait()
        flat = ring.reshape(slots, 2, contraction, head_dim)
        moves = [
            pltpu.make_async_copy(
                flat.at[slot, at],
                chunk.at[here, pl.ds(at * contraction, contraction)],
                tile_sems.at[at],
            )
            for at in range(2)
        ]
        for move in moves:
            move.start()

        for move in moves:
            move.wait()

        @pl.when(piece + slots < pieces)
        def _():
            for copy in bring(piece + slots, slot):
                copy.start()

        right = jnp.concatenate(
            [chunk[here, pl.ds(0, contraction)], chunk[here, pl.ds(contraction, contraction)]], axis=1
        )
        total = jnp.dot(left[...], right, preferred_element_type=f32)
        kept = lax.rem(piece, 3)
        own_sum[kept] = total.reshape(own_sum.shape[1:])
        core_send[piece] = own_sum[kept, 1 - core].astype(bf16)
        core_hop(piece).start()

        @pl.when(piece >= 2)
        def _():
            pass_on(piece - 2)

    pass_on(pieces - 2)
    pass_on(pieces - 1)
    square_hop.wait_recv()
    square_mid[...] = (square_all[core] + square_core[...]).reshape(square_mid.shape)
    square_recv[lane_at] = square_mid[mine]

    def square_send(off):
        other_lane = lax.rem(lane_at + off, lanes)
        return hop(
            square_mid.at[other_lane * head_devices + head],
            square_recv.at[lane_at],
            square_sems.at[2 + 2 * off],
            square_sems.at[3 + 2 * off],
            {"gx": other_lane * 2 + core},
        )

    def square_arrival(off):
        other_lane = lax.rem(lane_at + lanes - off, lanes)
        return hop(
            square_mid.at[mine],
            square_recv.at[other_lane],
            square_sems.at[2 + 2 * off],
            square_sems.at[3 + 2 * off],
            {"gx": other_lane * 2 + core},
        )

    for off in range(1, lanes):
        square_send(off).start()
    early = stretches // 2
    for at in range(early):
        weight_copy(at).start()

    stride = max_len + 16
    steps = 16
    kinds = 2 * all_groups
    size = steps * kinds
    to_row = lax.broadcasted_iota(jnp.int32, (size, size), 0)
    from_row = lax.broadcasted_iota(jnp.int32, (size, size), 1)
    regroup = jnp.where(
        from_row == lax.rem(to_row, steps) * kinds + to_row // steps, 1.0, 0.0
    ).astype(bf16)
    load_cache.wait()
    for row in range(rows_local):

        @pl.loop(0, max_len // (2 * steps))
        def _(step):
            first = pl.multiple_of(row * max_len * kinds + step * 2 * size, size)
            both = jnp.concatenate(
                [chunk[cache_slot, pl.ds(first, size)], chunk[cache_slot, pl.ds(first + size, size)]],
                axis=1,
            )
            sorted_rows = jnp.dot(regroup, both, preferred_element_type=f32).astype(bf16)
            for kind in range(kinds):
                base = (row * kinds + kind) * stride
                for half in range(2):
                    at = pl.multiple_of(base + (step * 2 + half) * steps, 16)
                    chunk[cached_slot, pl.ds(at, steps)] = sorted_rows[
                        kind * steps : (kind + 1) * steps, half * head_dim : (half + 1) * head_dim
                    ]

    row_at = lax.broadcasted_iota(jnp.int32, (block, head_dim), 0)
    lane = lax.broadcasted_iota(jnp.int32, (block, head_dim), 1)
    half_dim = head_dim // 2
    place = jnp.zeros((block, head_dim), jnp.int32)
    for row in range(rows_local):
        place = jnp.where(
            lax.rem(row_at, near) // pair == row, positions_ref[source_at * rows_local + row], place
        )
    place = (place + lax.rem(row_at, pair)).astype(f32)
    index_half = lax.rem(lane, half_dim).astype(f32)
    frequency = jnp.exp(index_half * (-2.0 * math.log(rope_base) / head_dim))
    angles = place * frequency
    cosine = jnp.cos(angles)
    sine = jnp.where(lane < half_dim, -jnp.sin(angles), jnp.sin(angles))

    for off in range(1, lanes):
        square_arrival(off).wait_recv()
    square_total = square_recv[0]
    for at in range(1, lanes):
        square_total = square_total + square_recv[at]
    inv_rms = lax.rsqrt(
        jnp.sum(square_total, axis=1, keepdims=True) / (local_width * places) + norm_eps
    )

    @pl.loop(0, pieces)
    def _(piece):
        for off in range(1, team):
            row_arrival(piece, off).wait_recv()

    small = lax.broadcasted_iota(jnp.int32, (block, head_dim), 0)
    for far in range(head_devices):
        for column in range(columns):
            piece, side = column // 2, column % 2
            value = row_recv[piece, far, :, side * head_dim : (side + 1) * head_dim].astype(f32)
            for at in range(1, lanes):
                value = value + row_recv[
                    piece, at * head_devices + far, :, side * head_dim : (side + 1) * head_dim
                ].astype(f32)
            value = value * inv_rms
            if column <= group_size:
                turned = jnp.concatenate([value[:, half_dim:], value[:, :half_dim]], axis=1)
                value = value * cosine + turned * sine
            if column < group_size:
                query_buf[far, column * block : (column + 1) * block, :] = value
            else:
                kind = column - group_size
                for group in range(groups):
                    for row in range(rows_local):
                        start = group * near + row * pair
                        moved = pltpu.roll(value, (block - start) % block, 0) if start else value
                        fresh = jnp.where(small < pair, moved, 0.0)
                        base = (
                            row * kinds + kind * all_groups + far * groups + group
                        ) * stride + max_len
                        chunk[cached_slot, pl.ds(base, 16)] = jnp.concatenate(
                            [fresh, jnp.zeros((16 - block, head_dim), f32)], axis=0
                        ).astype(bf16)

    scale_factor = 1.0 / math.sqrt(head_dim)
    count = pair * group_size
    slot_id = lax.broadcasted_iota(jnp.int32, (count, stride), 1)
    token_id = lax.broadcasted_iota(jnp.int32, (count, stride), 0) // group_size
    fresh_seen = (slot_id >= max_len) & (slot_id - max_len <= token_id)
    for row in range(rows_local):
        seen = (slot_id < lengths_ref[row]) | fresh_seen
        for every in range(all_groups):
            far, group = every // groups, every % groups
            first = group * near + row * pair
            queries = jnp.concatenate(
                [
                    query_buf[far, pl.ds(first + token, group_size, stride=block), :]
                    for token in range(pair)
                ],
                axis=0,
            ).astype(bf16)
            keys = chunk[cached_slot, pl.ds((row * kinds + every) * stride, stride)]
            values = chunk[cached_slot, pl.ds((row * kinds + all_groups + every) * stride, stride)]
            scores = lax.dot_general(
                queries, keys, (((1,), (1,)), ((), ())), preferred_element_type=f32
            )
            scores = jnp.where(seen, scores * scale_factor, -1e30)
            expo = jnp.exp(scores - jnp.max(scores, axis=1, keepdims=True))
            weight = (expo / jnp.sum(expo, axis=1, keepdims=True)).astype(bf16)
            result = jnp.dot(weight, values, preferred_element_type=f32)
            for token in range(pair):
                attended_buf[far, pl.ds(first + token, group_size, stride=block), :] = result[
                    token * group_size : (token + 1) * group_size
                ]
    for far in range(head_devices):
        for at in range(group_size):
            attended_send[far, :, at * head_dim : (at + 1) * head_dim] = attended_buf[
                far, at * block : (at + 1) * block, :
            ].astype(bf16)

    def att_hop(off):
        other, place_of = member(off)
        return hop(
            attended_send.at[place_of["gy"]],
            attended_recv.at[source_at],
            att_sends.at[other],
            att_recvs.at[mine],
            place_of,
        )

    def source_of(other, which):
        return ((other // head_devices) * 2 + which) * head_devices + lax.rem(other, head_devices)

    def att_arrival(off):
        other, place_of = member(off)
        return hop(
            attended_send.at[place_of["gy"]],
            attended_recv.at[source_of(other, core)],
            att_sends.at[other],
            att_recvs.at[other],
            place_of,
        )

    def pair_hop(other, which):
        from_at = source_of(other, which)
        return hop(
            attended_recv.at[from_at],
            attended_recv.at[from_at],
            pair_sends.at[other],
            pair_recvs.at[other],
            partner,
        )

    for off in range(team - 1, 0, -1):
        att_hop(off).start()
    attended_recv[source_at] = attended_send[head]
    pair_hop(mine, core).start()
    later = iter(range(early, stretches))
    for off in range(1, team):
        for at in itertools.islice(later, 2):
            weight_copy(at).start()
        att_arrival(off).wait_recv()
        pair_hop(lax.rem(mine + off, team), core).start()
    for at in later:
        weight_copy(at).start()
    for off in range(team):
        pair_hop(lax.rem(mine + off, team), 1 - core).wait_recv()

    heads_width = group_size * head_dim
    sources = places * head_devices
    first_rows = lax.rem(lax.broadcasted_iota(jnp.int32, (2 * block, heads_width), 0), block) // near
    for at in range(0, sources, 2):
        both = jnp.concatenate([attended_recv[at], attended_recv[at + 1]], axis=0).astype(f32)
        for group in range(groups):
            left[at * block : (at + 2) * block, group * heads_width : (group + 1) * heads_width] = (
                jnp.where(first_rows == group, both, 0.0).astype(bf16)
            )

    def part_hop(at, off):
        other = lax.rem(head + off, head_devices)
        return hop(
            part_send.at[at, other],
            part_recv.at[at, head],
            part_sends.at[at, other],
            part_recvs.at[at, head],
            {"gy": other},
        )

    def part_arrival(at, off):
        other = lax.rem(head + off, head_devices)
        return hop(
            part_send.at[at, other],
            part_recv.at[at, other],
            part_sends.at[at, other],
            part_recvs.at[at, other],
            {"gy": other},
        )

    across = part_own.shape[2]
    share = total_tokens // head_devices

    @pl.loop(0, stretches)
    def _(at):
        weight_copy(at).wait()
        span = pl.ds(pl.multiple_of(at * across, across), across)
        product = jnp.dot(
            left[:, : groups * heads_width], weights[:, span], preferred_element_type=f32
        )
        upper = lax.broadcasted_iota(jnp.int32, (block, across), 0) < near
        tiles = []
        for source in range(sources):
            tile = product[source * block : (source + 1) * block]
            tiles.append(tile + pltpu.roll(tile, near, 0))
        joined = [
            jnp.where(upper, tiles[source], tiles[source + 1]) for source in range(0, sources, 2)
        ]
        per = len(joined) // head_devices
        for far in range(head_devices):
            value = jnp.concatenate(joined[far * per : (far + 1) * per], axis=0)
            part_send[at, far] = value.astype(bf16)

            @pl.when(far == head)
            def _():
                part_own[at] = value

        for off in range(1, head_devices):
            part_hop(at, off).start()

    mine_rows = pl.ds(pl.multiple_of(head * share, share), share)

    @pl.loop(0, stretches)
    def _(at):
        span = pl.ds(pl.multiple_of(at * across, across), across)
        value = part_own[at] + tok[mine_rows, span].astype(f32)
        for off in range(1, head_devices):
            part_arrival(at, off).wait_recv()
            value = value + part_recv[at, lax.rem(head + off, head_devices)].astype(f32)
        for row in range(share // pair):
            for tile in range(across // 128):
                out_ref[row, at * (across // 128) + tile] = value[
                    row * pair : (row + 1) * pair, tile * 128 : (tile + 1) * 128
                ]

    square_hop.wait_send()
    for off in range(1, lanes):
        square_send(off).wait_send()

    @pl.loop(0, pieces)
    def _(piece):
        core_hop(piece).wait_send()
        for off in range(1, team):
            row_hop(piece, off).wait_send()

    for off in range(1, team):
        att_hop(off).wait_send()
    for off in range(team):
        pair_hop(lax.rem(mine + off, team), core).wait_send()

    @pl.loop(0, stretches)
    def _(at):
        for off in range(1, head_devices):
            part_hop(at, off).wait_send()


def whole_block(tokens, norm_gain, qkv_weight, out_weight, kv_cache, lengths, positions):
    f32, bf16 = jnp.float32, jnp.bfloat16
    rows_total, pair, local_width = tokens.shape
    groups, columns, head_dim = qkv_weight.shape[1:]
    places, head_devices = lax.axis_size("gx"), lax.axis_size("gy")
    rows_local, max_len = kv_cache.shape[:2]
    total_tokens = rows_total * pair
    group_size = columns - 2
    pieces = columns // 2
    slots = 3
    lanes = places // 2
    team = lanes * head_devices
    block = groups * rows_local * pair
    sources = places * head_devices
    share = total_tokens // head_devices
    across = 512
    stretches = local_width // across
    contraction = local_width * groups
    wide = 2 * head_dim
    hbm = pl.BlockSpec(memory_space=pl.ANY)
    smem = pl.BlockSpec(memory_space=pltpu.SMEM)
    dma = pltpu.SemaphoreType.DMA
    got = pl.pallas_call(
        functools.partial(block_kernel, head_devices, places),
        out_shape=jax.ShapeDtypeStruct((share // pair, local_width // 128, pair, 128), f32),
        in_specs=[hbm, hbm, hbm, hbm, hbm, smem, smem],
        out_specs=pl.BlockSpec(memory_space=pltpu.VMEM),
        scratch_shapes=[
            pltpu.VMEM((total_tokens, local_width), bf16),
            pltpu.VMEM((local_width // 128, 128), bf16),
            pltpu.VMEM((local_width // 128, 128), f32),
            pltpu.VMEM((total_tokens * groups, contraction), bf16),
            pltpu.VMEM((slots, 2, local_width, groups, head_dim), bf16),
            pltpu.VMEM((2, 2 * contraction, head_dim), bf16),
            pltpu.VMEM((out_weight.shape[0] * head_dim, local_width), bf16),
            pltpu.VMEM((3, 2, team * block, wide), f32),
            pltpu.VMEM((pieces, team * block, wide), bf16),
            pltpu.VMEM((pieces, team * block, wide), bf16),
            pltpu.VMEM((pieces, team, block, wide), bf16),
            pltpu.VMEM((pieces, team, block, wide), bf16),
            pltpu.VMEM((2, team * block, 128), f32),
            pltpu.VMEM((team * block, 128), f32),
            pltpu.VMEM((team, block, 128), f32),
            pltpu.VMEM((lanes, block, 128), f32),
            pltpu.VMEM((head_devices, group_size * block, head_dim), f32),
            pltpu.VMEM((head_devices, group_size * block, head_dim), f32),
            pltpu.VMEM((head_devices, block, group_size * head_dim), bf16),
            pltpu.VMEM((sources, block, group_size * head_dim), bf16),
            pltpu.VMEM((stretches, head_devices, share, across), bf16),
            pltpu.VMEM((stretches, head_devices, share, across), bf16),
            pltpu.VMEM((stretches, share, across), f32),
            dma((4,)),
            dma((slots, 2)),
            dma((2,)),
            dma((stretches,)),
            dma((2, pieces)),
            dma((pieces, team)),
            dma((pieces, team)),
            dma((2 + 2 * lanes,)),
            dma((team,)),
            dma((team,)),
            dma((team,)),
            dma((team,)),
            dma((stretches, head_devices)),
            dma((stretches, head_devices)),
        ],
        compiler_params=pltpu.CompilerParams(
            collective_id=0, has_side_effects=True, vmem_limit_bytes=63 << 20
        ),
    )(
        tokens,
        norm_gain.reshape(-1, 128),
        jnp.transpose(qkv_weight, (0, 2, 1, 3)),
        out_weight.reshape(-1, local_width),
        kv_cache.reshape(-1, head_dim),
        lengths,
        positions,
    )
    return jnp.transpose(got, (0, 2, 1, 3)).reshape(share // pair, pair, local_width)


def body(tokens, norm_gain, qkv_weight, out_weight, kv_cache, lengths, positions):
    rows_local = kv_cache.shape[0]
    head_devices = lax.axis_size("gy")
    width_index = lax.axis_index("gx")
    head_index = lax.axis_index("gy")
    total_rows = tokens.shape[0]
    local_width = tokens.shape[2]
    groups_local = qkv_weight.shape[1]
    group_width = qkv_weight.shape[2]
    head_dim = qkv_weight.shape[3]
    group_size = group_width - 2
    block_rows = rows_local * head_devices
    places = lax.axis_size("gx")
    pair = tokens.shape[1]
    contraction = local_width * groups_local
    resident = (
        out_weight.size
        + 10 * contraction * head_dim
        + total_rows * pair * (2 * local_width + groups_local * contraction)
    )
    if (
        groups_local * rows_local * pair == 8
        and places % 2 == 0
        and head_devices > 1
        and total_rows == rows_local * places * head_devices
        and places % head_devices == 0
        and group_width % 2 == 0
        and head_dim == 128
        and kv_cache.shape[1] % 32 == 0
        and local_width % 1024 == 0
        and 2 * resident < 59 << 20
    ):
        return whole_block(
            tokens, norm_gain, qkv_weight, out_weight, kv_cache, lengths, positions
        )
    tokens_wide = tokens.astype(jnp.float32)
    hidden = (tokens_wide * norm_gain.astype(jnp.float32)).astype(jnp.bfloat16)
    squares = jnp.sum(tokens_wide * tokens_wide, axis=-1)
    partial_value = jnp.dot(
        hidden.reshape(total_rows * 2, local_width),
        qkv_weight.reshape(local_width, -1),
        preferred_element_type=jnp.float32,
    )
    partial_value = partial_value.reshape(total_rows, 2, groups_local, group_width, head_dim)
    block_sum, block_squares = (
        lax.psum_scatter(partial_value, "gx", scatter_dimension=0, tiled=True),
        lax.psum_scatter(squares, "gx", scatter_dimension=0, tiled=True),
    )
    inv_rms = lax.rsqrt(block_squares / D + norm_eps)
    ready = finish(
        block_sum * inv_rms[:, :, None, None, None], positions, width_index * block_rows, block_rows
    )
    packed = lax.all_to_all(ready, "gy", split_axis=0, concat_axis=2, tiled=True)
    queries = packed[:, :, :, :group_size]
    key_new = packed[:, :, :, group_size]
    value_new = packed[:, :, :, group_size + 1]
    attended = attend(queries, key_new, value_new, kv_cache, lengths)
    regrouped = lax.all_to_all(attended, "gy", split_axis=2, concat_axis=0, tiled=True)
    out_flat = out_weight.reshape(-1, local_width)
    row_piece = lax.all_gather(regrouped, "gx", axis=0, tiled=True)
    piece_rows = row_piece.shape[0]
    product = jnp.dot(
        row_piece.reshape(piece_rows * 2, -1), out_flat, preferred_element_type=jnp.float32
    )
    terms = product.astype(jnp.bfloat16).reshape(head_devices, -1, 2, local_width)
    arrived = lax.all_to_all(terms, "gy", split_axis=0, concat_axis=0)
    own_sum = jnp.sum(arrived.astype(jnp.float32), axis=0)
    row_share = total_rows // head_devices
    residual = lax.dynamic_slice_in_dim(tokens, head_index * row_share, row_share, 0).astype(
        jnp.float32
    )
    return residual + own_sum


def solution(mesh):
    return jax.shard_map(
        body,
        mesh=mesh,
        in_specs=(
            P("groups", None, "gx"),
            P("gx"),
            P("gx", "gy", None, None),
            P("gy", None, "gx"),
            P(("groups", "gx", "gy"), None, None, None, None),
            P(("groups", "gx", "gy")),
            P("groups"),
        ),
        out_specs=P(("groups", "gy"), None, "gx"),
        check_vma=False,
    )
```

```python
import functools
import itertools
import math

import jax
import jax.numpy as jnp
from jax import lax
from jax.experimental import pallas as pl
from jax.experimental.pallas import tpu as pltpu
from jax.sharding import PartitionSpec as P

D = 16384


norm_eps = 1e-05
rope_base = 500000.0


def rotate(values, places):
    half_dim = values.shape[-1] // 2
    index_half = jnp.arange(half_dim, dtype=jnp.float32)
    frequency = rope_base ** (-2.0 * index_half / values.shape[-1])
    angles = places[..., None] * frequency
    cosine = jnp.cos(angles)
    sine_part = jnp.sin(angles)
    front_half = values[..., :half_dim]
    back_half = values[..., half_dim:]
    return jnp.concatenate(
        [front_half * cosine - back_half * sine_part, back_half * cosine + front_half * sine_part],
        axis=-1,
    )


def finish(projected, positions, first_row, row_count):
    group_size = projected.shape[3] - 2
    placed = lax.dynamic_slice_in_dim(positions, first_row, row_count, 0)
    places = (placed[:, None] + jnp.arange(2, dtype=jnp.int32)[None, :]).astype(jnp.float32)
    queries = rotate(projected[:, :, :, :group_size], places[:, :, None, None])
    key_new = rotate(projected[:, :, :, group_size : group_size + 1], places[:, :, None, None])
    value_new = projected[:, :, :, group_size + 1 :]
    return jnp.concatenate([queries, key_new, value_new], axis=3).astype(jnp.bfloat16)


def attend(queries, key_new, value_new, cache_rows, length):
    scale_factor = 1.0 / math.sqrt(queries.shape[-1])
    scores_old = (
        jnp.einsum(
            "rtgid,rsgd->rtgis", queries, cache_rows[:, :, 0], preferred_element_type=jnp.float32
        )
        * scale_factor
    )
    slot_ids = jnp.arange(cache_rows.shape[1], dtype=jnp.int32)
    visible = slot_ids[None, :] < length[:, None]
    scores_old = jnp.where(visible[:, None, None, None, :], scores_old, -1e30)
    scores_new = (
        jnp.einsum("rtgid,rugd->rtgiu", queries, key_new, preferred_element_type=jnp.float32)
        * scale_factor
    )
    token_ids = jnp.arange(queries.shape[1], dtype=jnp.int32)
    causal = token_ids[:, None] >= token_ids[None, :]
    scores_new = jnp.where(causal[None, :, None, None, :], scores_new, -1e30)
    highest = jnp.maximum(jnp.max(scores_old, axis=-1), jnp.max(scores_new, axis=-1))
    expo_old = jnp.exp(scores_old - highest[..., None])
    expo_new = jnp.exp(scores_new - highest[..., None])
    denominator = jnp.sum(expo_old, axis=-1) + jnp.sum(expo_new, axis=-1)
    weight_old = (expo_old / denominator[..., None]).astype(jnp.bfloat16)
    weight_new = (expo_new / denominator[..., None]).astype(jnp.bfloat16)
    attended = jnp.einsum(
        "rtgis,rsgd->rtgid", weight_old, cache_rows[:, :, 1], preferred_element_type=jnp.float32
    )
    attended = attended + jnp.einsum(
        "rtgiu,rugd->rtgid", weight_new, value_new, preferred_element_type=jnp.float32
    )
    return attended.astype(jnp.bfloat16)


def hop(source, target, sends, arrivals, place):
    return pltpu.make_async_remote_copy(
        src_ref=source,
        dst_ref=target,
        send_sem=sends,
        recv_sem=arrivals,
        device_id=place,
        device_id_type=pl.DeviceIdType.MESH,
    )


def block_kernel(
    head_devices,
    places,
    tokens_ref,
    gain_ref,
    qkv_ref,
    out_weight_ref,
    cache_ref,
    lengths_ref,
    positions_ref,
    out_ref,
    tok,
    gain,
    gain_wide,
    left,
    ring,
    chunk,
    weights,
    own_sum,
    core_send,
    core_recv,
    row_send,
    row_recv,
    square_all,
    square_core,
    square_mid,
    square_recv,
    query_buf,
    attended_buf,
    attended_send,
    attended_recv,
    part_send,
    part_recv,
    part_own,
    load_sems,
    ring_sems,
    tile_sems,
    weight_sems,
    core_sems,
    row_sends,
    row_recvs,
    square_sems,
    att_sends,
    att_recvs,
    pair_sends,
    pair_recvs,
    part_sends,
    part_recvs,
):
    f32, bf16 = jnp.float32, jnp.bfloat16
    rows_total, pair, local_width = tokens_ref.shape
    total_tokens = rows_total * pair
    columns, head_dim = qkv_ref.shape[1], qkv_ref.shape[3]
    groups = qkv_ref.shape[2]
    group_size = columns - 2
    pieces = columns // 2
    slots = ring.shape[0]
    max_len = (cache_ref.shape[0] // (2 * groups * head_devices)) // lengths_ref.shape[0]
    rows_local = lengths_ref.shape[0]
    all_groups = groups * head_devices
    near = rows_local * pair
    block = groups * near
    lanes = places // 2
    team = lanes * head_devices
    contraction = local_width * groups
    width = lax.axis_index("gx")
    head = lax.axis_index("gy")
    core = lax.rem(width, 2)
    lane_at = width // 2
    mine = lane_at * head_devices + head
    source_at = width * head_devices + head
    partner = {"gx": width + 1 - 2 * core}

    def member(off):
        other = lax.rem(mine + off, team)
        far_lane, far_head = other // head_devices, lax.rem(other, head_devices)
        return other, {"gx": far_lane * 2 + core, "gy": far_head}

    def bring(piece, slot):
        return [
            pltpu.make_async_copy(
                qkv_ref.at[:, piece * 2 + at], ring.at[slot, at], ring_sems.at[slot, at]
            )
            for at in range(2)
        ]

    load_tokens = pltpu.make_async_copy(
        tokens_ref.reshape(total_tokens, local_width), tok, load_sems.at[0]
    )
    load_gain = pltpu.make_async_copy(gain_ref, gain, load_sems.at[1])
    load_tokens.start()
    load_gain.start()
    for piece in range(min(slots, pieces)):
        for copy in bring(piece, piece):
            copy.start()
    barrier = pltpu.get_barrier_semaphore()
    pl.semaphore_signal(barrier, inc=1, device_id=partner, device_id_type=pl.DeviceIdType.MESH)
    for off in range(1, team):
        pl.semaphore_signal(
            barrier, inc=1, device_id=member(off)[1], device_id_type=pl.DeviceIdType.MESH
        )

    made = lax.broadcasted_iota(jnp.int32, (total_tokens * groups, total_tokens), 0)
    held = lax.broadcasted_iota(jnp.int32, (total_tokens * groups, total_tokens), 1)
    target = made // block
    owner_core = target // team
    owner_lane = lax.rem(target, team) // head_devices
    owner_head = lax.rem(target, head_devices)
    owner = (owner_lane * 2 + owner_core) * head_devices + owner_head
    chosen = owner * near + lax.rem(made, near) == held
    chooser = jnp.where(chosen, 1.0, 0.0)
    group_row = lax.rem(
        lax.broadcasted_iota(jnp.int32, (total_tokens * groups, 128), 0), block
    ) // near
    feature = lax.broadcasted_iota(jnp.int32, (128 * groups, 128 * groups), 0)
    goal = lax.broadcasted_iota(jnp.int32, (128 * groups, 128 * groups), 1)
    spread = jnp.where(
        goal == lax.rem(feature, 128) * groups + feature // 128, 1.0, 0.0
    ).astype(bf16)

    load_tokens.wait()
    load_gain.wait()
    gain_wide[...] = gain[...].astype(f32)
    depth = 1024

    def widen(at, squares):
        start = pl.multiple_of(at * depth, depth)
        wide = tok[:, pl.ds(start, depth)].astype(f32)
        scale = jnp.concatenate(
            [gain_wide[pl.ds(at * (depth // 128) + q, 1), :] for q in range(depth // 128)], axis=1
        )
        hidden = (wide * scale).astype(bf16)
        ordered = jnp.dot(chooser.astype(bf16), hidden, preferred_element_type=f32)
        for q in range(depth // 128):
            part = wide[:, q * 128 : (q + 1) * 128]
            squares += part * part
            near_part = ordered[:, q * 128 : (q + 1) * 128]
            split = jnp.concatenate(
                [jnp.where(group_row == group, near_part, 0.0) for group in range(groups)], axis=1
            ).astype(bf16)
            begin = pl.multiple_of((start + q * 128) * groups, 128 * groups)
            left[:, pl.ds(begin, 128 * groups)] = jnp.dot(
                split, spread, preferred_element_type=f32
            ).astype(bf16)
        return squares

    squares = lax.fori_loop(
        0, local_width // depth, widen, jnp.zeros((total_tokens, 128), f32)
    )
    square_all[...] = jnp.dot(
        chooser, squares, preferred_element_type=f32, precision=lax.Precision.HIGHEST
    ).reshape(square_all.shape)
    pl.semaphore_wait(barrier, team)

    square_hop = hop(
        square_all.at[1 - core], square_core, square_sems.at[0], square_sems.at[1], partner
    )
    square_hop.start()

    def core_hop(piece):
        return hop(
            core_send.at[piece],
            core_recv.at[piece],
            core_sems.at[0, piece],
            core_sems.at[1, piece],
            partner,
        )

    def row_hop(piece, off):
        other, place = member(off)
        return hop(
            row_send.at[piece, other],
            row_recv.at[piece, mine],
            row_sends.at[piece, other],
            row_recvs.at[piece, mine],
            place,
        )

    def row_arrival(piece, off):
        other, place = member(off)
        return hop(
            row_send.at[piece, other],
            row_recv.at[piece, other],
            row_sends.at[piece, other],
            row_recvs.at[piece, other],
            place,
        )

    def pass_on(piece):
        core_hop(piece).wait_recv()
        total = own_sum[lax.rem(piece, 3), core] + core_recv[piece].astype(f32)
        row_send[piece] = total.reshape(row_send.shape[1:]).astype(bf16)
        row_recv[piece, mine] = row_send[piece, mine]
        for off in range(1, team):
            row_hop(piece, off).start()

    def weight_copy(at):
        across = part_own.shape[2]
        return pltpu.make_async_copy(
            out_weight_ref.at[:, pl.ds(at * across, across)],
            weights.at[:, pl.ds(at * across, across)],
            weight_sems.at[at],
        )

    stretches = part_own.shape[0]
    cache_slot, cached_slot = pieces % 2, (pieces - 1) % 2
    cache_rows = cache_ref.shape[0]
    load_cache = pltpu.make_async_copy(
        cache_ref, chunk.at[cache_slot, pl.ds(0, cache_rows)], load_sems.at[3]
    )

    @pl.loop(0, pieces)
    def _(piece):
        slot, here = lax.rem(piece, slots), lax.rem(piece, 2)

        @pl.when(piece == pieces - 1)
        def _():
            load_cache.start()

        for copy in bring(piece, slot):
            copy.wait()
        flat = ring.reshape(slots, 2, contraction, head_dim)
        moves = [
            pltpu.make_async_copy(
                flat.at[slot, at],
                chunk.at[here, pl.ds(at * contraction, contraction)],
                tile_sems.at[at],
            )
            for at in range(2)
        ]
        for move in moves:
            move.start()

        for move in moves:
            move.wait()

        @pl.when(piece + slots < pieces)
        def _():
            for copy in bring(piece + slots, slot):
                copy.start()

        right = jnp.concatenate(
            [chunk[here, pl.ds(0, contraction)], chunk[here, pl.ds(contraction, contraction)]], axis=1
        )
        total = jnp.dot(left[...], right, preferred_element_type=f32)
        kept = lax.rem(piece, 3)
        own_sum[kept] = total.reshape(own_sum.shape[1:])
        core_send[piece] = own_sum[kept, 1 - core].astype(bf16)
        core_hop(piece).start()

        @pl.when(piece >= 2)
        def _():
            pass_on(piece - 2)

    pass_on(pieces - 2)
    pass_on(pieces - 1)
    square_hop.wait_recv()
    square_mid[...] = (square_all[core] + square_core[...]).reshape(square_mid.shape)
    square_recv[lane_at] = square_mid[mine]

    def square_send(off):
        other_lane = lax.rem(lane_at + off, lanes)
        return hop(
            square_mid.at[other_lane * head_devices + head],
            square_recv.at[lane_at],
            square_sems.at[2 + 2 * off],
            square_sems.at[3 + 2 * off],
            {"gx": other_lane * 2 + core},
        )

    def square_arrival(off):
        other_lane = lax.rem(lane_at + lanes - off, lanes)
        return hop(
            square_mid.at[mine],
            square_recv.at[other_lane],
            square_sems.at[2 + 2 * off],
            square_sems.at[3 + 2 * off],
            {"gx": other_lane * 2 + core},
        )

    for off in range(1, lanes):
        square_send(off).start()
    early = stretches // 2
    for at in range(early):
        weight_copy(at).start()

    stride = max_len + 16
    steps = 16
    kinds = 2 * all_groups
    size = steps * kinds
    to_row = lax.broadcasted_iota(jnp.int32, (size, size), 0)
    from_row = lax.broadcasted_iota(jnp.int32, (size, size), 1)
    regroup = jnp.where(
        from_row == lax.rem(to_row, steps) * kinds + to_row // steps, 1.0, 0.0
    ).astype(bf16)
    load_cache.wait()
    for row in range(rows_local):

        @pl.loop(0, max_len // (2 * steps))
        def _(step):
            first = pl.multiple_of(row * max_len * kinds + step * 2 * size, size)
            both = jnp.concatenate(
                [chunk[cache_slot, pl.ds(first, size)], chunk[cache_slot, pl.ds(first + size, size)]],
                axis=1,
            )
            sorted_rows = jnp.dot(regroup, both, preferred_element_type=f32).astype(bf16)
            for kind in range(kinds):
                base = (row * kinds + kind) * stride
                for half in range(2):
                    at = pl.multiple_of(base + (step * 2 + half) * steps, 16)
                    chunk[cached_slot, pl.ds(at, steps)] = sorted_rows[
                        kind * steps : (kind + 1) * steps, half * head_dim : (half + 1) * head_dim
                    ]

    row_at = lax.broadcasted_iota(jnp.int32, (block, head_dim), 0)
    lane = lax.broadcasted_iota(jnp.int32, (block, head_dim), 1)
    half_dim = head_dim // 2
    place = jnp.zeros((block, head_dim), jnp.int32)
    for row in range(rows_local):
        place = jnp.where(
            lax.rem(row_at, near) // pair == row, positions_ref[source_at * rows_local + row], place
        )
    place = (place + lax.rem(row_at, pair)).astype(f32)
    index_half = lax.rem(lane, half_dim).astype(f32)
    frequency = jnp.exp(index_half * (-2.0 * math.log(rope_base) / head_dim))
    angles = place * frequency
    cosine = jnp.cos(angles)
    sine = jnp.where(lane < half_dim, -jnp.sin(angles), jnp.sin(angles))

    for off in range(1, lanes):
        square_arrival(off).wait_recv()
    square_total = square_recv[0]
    for at in range(1, lanes):
        square_total = square_total + square_recv[at]
    inv_rms = lax.rsqrt(
        jnp.sum(square_total, axis=1, keepdims=True) / (local_width * places) + norm_eps
    )

    @pl.loop(0, pieces)
    def _(piece):
        for off in range(1, team):
            row_arrival(piece, off).wait_recv()

    small = lax.broadcasted_iota(jnp.int32, (block, head_dim), 0)
    scale_factor = 1.0 / math.sqrt(head_dim)
    count = pair * group_size
    slot_id = lax.broadcasted_iota(jnp.int32, (count, stride), 1)
    token_id = lax.broadcasted_iota(jnp.int32, (count, stride), 0) // group_size
    fresh_seen = (slot_id >= max_len) & (slot_id - max_len <= token_id)

    def send_to(far, at):
        other = at * head_devices + far

        @pl.when(other != mine)
        def _():
            hop(
                attended_send.at[far],
                attended_recv.at[source_at],
                att_sends.at[other],
                att_recvs.at[mine],
                {"gx": at * 2 + core, "gy": far},
            ).start()

        @pl.when(other == mine)
        def _():
            attended_recv[source_at] = attended_send[far]

    ends = [
        far
        for near_end in range((head_devices + 1) // 2)
        for far in sorted({near_end, head_devices - 1 - near_end})
    ]
    for far in ends:
        for column in range(columns):
            piece, side = column // 2, column % 2
            value = row_recv[piece, far, :, side * head_dim : (side + 1) * head_dim].astype(f32)
            for at in range(1, lanes):
                value = value + row_recv[
                    piece, at * head_devices + far, :, side * head_dim : (side + 1) * head_dim
                ].astype(f32)
            value = value * inv_rms
            if column <= group_size:
                turned = jnp.concatenate([value[:, half_dim:], value[:, :half_dim]], axis=1)
                value = value * cosine + turned * sine
            if column < group_size:
                query_buf[far, column * block : (column + 1) * block, :] = value
            else:
                kind = column - group_size
                for group in range(groups):
                    for row in range(rows_local):
                        start = group * near + row * pair
                        moved = pltpu.roll(value, (block - start) % block, 0) if start else value
                        fresh = jnp.where(small < pair, moved, 0.0)
                        base = (
                            row * kinds + kind * all_groups + far * groups + group
                        ) * stride + max_len
                        chunk[cached_slot, pl.ds(base, 16)] = jnp.concatenate(
                            [fresh, jnp.zeros((16 - block, head_dim), f32)], axis=0
                        ).astype(bf16)
        for row in range(rows_local):
            seen = (slot_id < lengths_ref[row]) | fresh_seen
            for group in range(groups):
                every = far * groups + group
                first = group * near + row * pair
                queries = jnp.concatenate(
                    [
                        query_buf[far, pl.ds(first + token, group_size, stride=block), :]
                        for token in range(pair)
                    ],
                    axis=0,
                ).astype(bf16)
                keys = chunk[cached_slot, pl.ds((row * kinds + every) * stride, stride)]
                values = chunk[
                    cached_slot, pl.ds((row * kinds + all_groups + every) * stride, stride)
                ]
                scores = lax.dot_general(
                    queries, keys, (((1,), (1,)), ((), ())), preferred_element_type=f32
                )
                scores = jnp.where(seen, scores * scale_factor, -1e30)
                expo = jnp.exp(scores - jnp.max(scores, axis=1, keepdims=True))
                weight = (expo / jnp.sum(expo, axis=1, keepdims=True)).astype(bf16)
                result = jnp.dot(weight, values, preferred_element_type=f32)
                for token in range(pair):
                    attended_buf[far, pl.ds(first + token, group_size, stride=block), :] = result[
                        token * group_size : (token + 1) * group_size
                    ]
        for at in range(group_size):
            attended_send[far, :, at * head_dim : (at + 1) * head_dim] = attended_buf[
                far, at * block : (at + 1) * block, :
            ].astype(bf16)
        for at in range(lanes):
            send_to(far, at)

    def att_hop(off):
        other, place_of = member(off)
        return hop(
            attended_send.at[place_of["gy"]],
            attended_recv.at[source_at],
            att_sends.at[other],
            att_recvs.at[mine],
            place_of,
        )

    def source_of(other, which):
        return ((other // head_devices) * 2 + which) * head_devices + lax.rem(other, head_devices)

    def att_arrival(off):
        other, place_of = member(off)
        return hop(
            attended_send.at[place_of["gy"]],
            attended_recv.at[source_of(other, core)],
            att_sends.at[other],
            att_recvs.at[other],
            place_of,
        )

    def pair_hop(other, which):
        from_at = source_of(other, which)
        return hop(
            attended_recv.at[from_at],
            attended_recv.at[from_at],
            pair_sends.at[other],
            pair_recvs.at[other],
            partner,
        )

    pair_hop(mine, core).start()
    later = iter(range(early, stretches))
    for off in range(1, team):
        for at in itertools.islice(later, 2):
            weight_copy(at).start()
        att_arrival(off).wait_recv()
        pair_hop(lax.rem(mine + off, team), core).start()
    for at in later:
        weight_copy(at).start()
    for off in range(team):
        pair_hop(lax.rem(mine + off, team), 1 - core).wait_recv()

    heads_width = group_size * head_dim
    sources = places * head_devices
    first_rows = lax.rem(lax.broadcasted_iota(jnp.int32, (2 * block, heads_width), 0), block) // near
    for at in range(0, sources, 2):
        both = jnp.concatenate([attended_recv[at], attended_recv[at + 1]], axis=0).astype(f32)
        for group in range(groups):
            left[at * block : (at + 2) * block, group * heads_width : (group + 1) * heads_width] = (
                jnp.where(first_rows == group, both, 0.0).astype(bf16)
            )

    def part_hop(at, off):
        other = lax.rem(head + off, head_devices)
        return hop(
            part_send.at[at, other],
            part_recv.at[at, head],
            part_sends.at[at, other],
            part_recvs.at[at, head],
            {"gy": other},
        )

    def part_arrival(at, off):
        other = lax.rem(head + off, head_devices)
        return hop(
            part_send.at[at, other],
            part_recv.at[at, other],
            part_sends.at[at, other],
            part_recvs.at[at, other],
            {"gy": other},
        )

    across = part_own.shape[2]
    share = total_tokens // head_devices

    @pl.loop(0, stretches)
    def _(at):
        weight_copy(at).wait()
        span = pl.ds(pl.multiple_of(at * across, across), across)
        product = jnp.dot(
            left[:, : groups * heads_width], weights[:, span], preferred_element_type=f32
        )
        upper = lax.broadcasted_iota(jnp.int32, (block, across), 0) < near
        tiles = []
        for source in range(sources):
            tile = product[source * block : (source + 1) * block]
            tiles.append(tile + pltpu.roll(tile, near, 0))
        joined = [
            jnp.where(upper, tiles[source], tiles[source + 1]) for source in range(0, sources, 2)
        ]
        per = len(joined) // head_devices
        for far in range(head_devices):
            value = jnp.concatenate(joined[far * per : (far + 1) * per], axis=0)
            part_send[at, far] = value.astype(bf16)

            @pl.when(far == head)
            def _():
                part_own[at] = value

        for off in range(1, head_devices):
            part_hop(at, off).start()

    mine_rows = pl.ds(pl.multiple_of(head * share, share), share)

    @pl.loop(0, stretches)
    def _(at):
        span = pl.ds(pl.multiple_of(at * across, across), across)
        value = part_own[at] + tok[mine_rows, span].astype(f32)
        for off in range(1, head_devices):
            part_arrival(at, off).wait_recv()
            value = value + part_recv[at, lax.rem(head + off, head_devices)].astype(f32)
        for row in range(share // pair):
            for tile in range(across // 128):
                out_ref[row, at * (across // 128) + tile] = value[
                    row * pair : (row + 1) * pair, tile * 128 : (tile + 1) * 128
                ]

    square_hop.wait_send()
    for off in range(1, lanes):
        square_send(off).wait_send()

    @pl.loop(0, pieces)
    def _(piece):
        core_hop(piece).wait_send()
        for off in range(1, team):
            row_hop(piece, off).wait_send()

    for off in range(1, team):
        att_hop(off).wait_send()
    for off in range(team):
        pair_hop(lax.rem(mine + off, team), core).wait_send()

    @pl.loop(0, stretches)
    def _(at):
        for off in range(1, head_devices):
            part_hop(at, off).wait_send()


def store_kernel(value_ref, out_ref, sem):
    copy = pltpu.make_async_copy(value_ref, out_ref, sem.at[0])
    copy.start()
    copy.wait()


def whole_block(tokens, norm_gain, qkv_weight, out_weight, kv_cache, lengths, positions):
    f32, bf16 = jnp.float32, jnp.bfloat16
    rows_total, pair, local_width = tokens.shape
    groups, columns, head_dim = qkv_weight.shape[1:]
    places, head_devices = lax.axis_size("gx"), lax.axis_size("gy")
    rows_local, max_len = kv_cache.shape[:2]
    total_tokens = rows_total * pair
    group_size = columns - 2
    pieces = columns // 2
    slots = 3
    lanes = places // 2
    team = lanes * head_devices
    block = groups * rows_local * pair
    sources = places * head_devices
    share = total_tokens // head_devices
    across = 512
    stretches = local_width // across
    contraction = local_width * groups
    wide = 2 * head_dim
    hbm = pl.BlockSpec(memory_space=pl.ANY)
    smem = pl.BlockSpec(memory_space=pltpu.SMEM)
    dma = pltpu.SemaphoreType.DMA
    got = pl.pallas_call(
        functools.partial(block_kernel, head_devices, places),
        out_shape=jax.ShapeDtypeStruct((share // pair, local_width // 128, pair, 128), f32),
        in_specs=[hbm, hbm, hbm, hbm, hbm, smem, smem],
        out_specs=pl.BlockSpec(memory_space=pltpu.VMEM),
        scratch_shapes=[
            pltpu.VMEM((total_tokens, local_width), bf16),
            pltpu.VMEM((local_width // 128, 128), bf16),
            pltpu.VMEM((local_width // 128, 128), f32),
            pltpu.VMEM((total_tokens * groups, contraction), bf16),
            pltpu.VMEM((slots, 2, local_width, groups, head_dim), bf16),
            pltpu.VMEM((2, 2 * contraction, head_dim), bf16),
            pltpu.VMEM((out_weight.shape[0] * head_dim, local_width), bf16),
            pltpu.VMEM((3, 2, team * block, wide), f32),
            pltpu.VMEM((pieces, team * block, wide), bf16),
            pltpu.VMEM((pieces, team * block, wide), bf16),
            pltpu.VMEM((pieces, team, block, wide), bf16),
            pltpu.VMEM((pieces, team, block, wide), bf16),
            pltpu.VMEM((2, team * block, 128), f32),
            pltpu.VMEM((team * block, 128), f32),
            pltpu.VMEM((team, block, 128), f32),
            pltpu.VMEM((lanes, block, 128), f32),
            pltpu.VMEM((head_devices, group_size * block, head_dim), f32),
            pltpu.VMEM((head_devices, group_size * block, head_dim), f32),
            pltpu.VMEM((head_devices, block, group_size * head_dim), bf16),
            pltpu.VMEM((sources, block, group_size * head_dim), bf16),
            pltpu.VMEM((stretches, head_devices, share, across), bf16),
            pltpu.VMEM((stretches, head_devices, share, across), bf16),
            pltpu.VMEM((stretches, share, across), f32),
            dma((4,)),
            dma((slots, 2)),
            dma((2,)),
            dma((stretches,)),
            dma((2, pieces)),
            dma((pieces, team)),
            dma((pieces, team)),
            dma((2 + 2 * lanes,)),
            dma((team,)),
            dma((team,)),
            dma((team,)),
            dma((team,)),
            dma((stretches, head_devices)),
            dma((stretches, head_devices)),
        ],
        compiler_params=pltpu.CompilerParams(
            collective_id=0, has_side_effects=True, vmem_limit_bytes=60 << 20
        ),
    )(
        tokens,
        norm_gain.reshape(-1, 128),
        jnp.transpose(qkv_weight, (0, 2, 1, 3)),
        out_weight.reshape(-1, local_width),
        kv_cache.reshape(-1, head_dim),
        lengths,
        positions,
    )
    got = pl.pallas_call(
        store_kernel,
        out_shape=jax.ShapeDtypeStruct(got.shape, f32),
        in_specs=[pl.BlockSpec(memory_space=pltpu.VMEM)],
        out_specs=hbm,
        scratch_shapes=[dma((1,))],
    )(got)
    return jnp.transpose(got, (0, 2, 1, 3)).reshape(share // pair, pair, local_width)


def body(tokens, norm_gain, qkv_weight, out_weight, kv_cache, lengths, positions):
    rows_local = kv_cache.shape[0]
    head_devices = lax.axis_size("gy")
    width_index = lax.axis_index("gx")
    head_index = lax.axis_index("gy")
    total_rows = tokens.shape[0]
    local_width = tokens.shape[2]
    groups_local = qkv_weight.shape[1]
    group_width = qkv_weight.shape[2]
    head_dim = qkv_weight.shape[3]
    group_size = group_width - 2
    block_rows = rows_local * head_devices
    places = lax.axis_size("gx")
    pair = tokens.shape[1]
    contraction = local_width * groups_local
    resident = (
        out_weight.size
        + 10 * contraction * head_dim
        + total_rows * pair * (2 * local_width + groups_local * contraction)
    )
    if (
        groups_local * rows_local * pair == 8
        and places % 2 == 0
        and head_devices > 1
        and total_rows == rows_local * places * head_devices
        and places % head_devices == 0
        and group_width % 2 == 0
        and head_dim == 128
        and kv_cache.shape[1] % 32 == 0
        and local_width % 1024 == 0
        and 2 * resident < 59 << 20
    ):
        return whole_block(
            tokens, norm_gain, qkv_weight, out_weight, kv_cache, lengths, positions
        )
    tokens_wide = tokens.astype(jnp.float32)
    hidden = (tokens_wide * norm_gain.astype(jnp.float32)).astype(jnp.bfloat16)
    squares = jnp.sum(tokens_wide * tokens_wide, axis=-1)
    partial_value = jnp.dot(
        hidden.reshape(total_rows * 2, local_width),
        qkv_weight.reshape(local_width, -1),
        preferred_element_type=jnp.float32,
    )
    partial_value = partial_value.reshape(total_rows, 2, groups_local, group_width, head_dim)
    block_sum, block_squares = (
        lax.psum_scatter(partial_value, "gx", scatter_dimension=0, tiled=True),
        lax.psum_scatter(squares, "gx", scatter_dimension=0, tiled=True),
    )
    inv_rms = lax.rsqrt(block_squares / D + norm_eps)
    ready = finish(
        block_sum * inv_rms[:, :, None, None, None], positions, width_index * block_rows, block_rows
    )
    packed = lax.all_to_all(ready, "gy", split_axis=0, concat_axis=2, tiled=True)
    queries = packed[:, :, :, :group_size]
    key_new = packed[:, :, :, group_size]
    value_new = packed[:, :, :, group_size + 1]
    attended = attend(queries, key_new, value_new, kv_cache, lengths)
    regrouped = lax.all_to_all(attended, "gy", split_axis=2, concat_axis=0, tiled=True)
    out_flat = out_weight.reshape(-1, local_width)
    row_piece = lax.all_gather(regrouped, "gx", axis=0, tiled=True)
    piece_rows = row_piece.shape[0]
    product = jnp.dot(
        row_piece.reshape(piece_rows * 2, -1), out_flat, preferred_element_type=jnp.float32
    )
    terms = product.astype(jnp.bfloat16).reshape(head_devices, -1, 2, local_width)
    arrived = lax.all_to_all(terms, "gy", split_axis=0, concat_axis=0)
    own_sum = jnp.sum(arrived.astype(jnp.float32), axis=0)
    row_share = total_rows // head_devices
    residual = lax.dynamic_slice_in_dim(tokens, head_index * row_share, row_share, 0).astype(
        jnp.float32
    )
    return residual + own_sum


def solution(mesh):
    return jax.shard_map(
        body,
        mesh=mesh,
        in_specs=(
            P("groups", None, "gx"),
            P("gx"),
            P("gx", "gy", None, None),
            P("gy", None, "gx"),
            P(("groups", "gx", "gy"), None, None, None, None),
            P(("groups", "gx", "gy")),
            P("groups"),
        ),
        out_specs=P(("groups", "gy"), None, "gx"),
        check_vma=False,
    )
```

```python
import functools
import itertools
import math

import jax
import jax.numpy as jnp
from jax import lax
from jax.experimental import pallas as pl
from jax.experimental.pallas import tpu as pltpu
from jax.sharding import PartitionSpec as P

D = 16384


norm_eps = 1e-05
rope_base = 500000.0


def rotate(values, places):
    half_dim = values.shape[-1] // 2
    index_half = jnp.arange(half_dim, dtype=jnp.float32)
    frequency = rope_base ** (-2.0 * index_half / values.shape[-1])
    angles = places[..., None] * frequency
    cosine = jnp.cos(angles)
    sine_part = jnp.sin(angles)
    front_half = values[..., :half_dim]
    back_half = values[..., half_dim:]
    return jnp.concatenate(
        [front_half * cosine - back_half * sine_part, back_half * cosine + front_half * sine_part],
        axis=-1,
    )


def finish(projected, positions, first_row, row_count):
    group_size = projected.shape[3] - 2
    placed = lax.dynamic_slice_in_dim(positions, first_row, row_count, 0)
    places = (placed[:, None] + jnp.arange(2, dtype=jnp.int32)[None, :]).astype(jnp.float32)
    queries = rotate(projected[:, :, :, :group_size], places[:, :, None, None])
    key_new = rotate(projected[:, :, :, group_size : group_size + 1], places[:, :, None, None])
    value_new = projected[:, :, :, group_size + 1 :]
    return jnp.concatenate([queries, key_new, value_new], axis=3).astype(jnp.bfloat16)


def attend(queries, key_new, value_new, cache_rows, length):
    scale_factor = 1.0 / math.sqrt(queries.shape[-1])
    scores_old = (
        jnp.einsum(
            "rtgid,rsgd->rtgis", queries, cache_rows[:, :, 0], preferred_element_type=jnp.float32
        )
        * scale_factor
    )
    slot_ids = jnp.arange(cache_rows.shape[1], dtype=jnp.int32)
    visible = slot_ids[None, :] < length[:, None]
    scores_old = jnp.where(visible[:, None, None, None, :], scores_old, -1e30)
    scores_new = (
        jnp.einsum("rtgid,rugd->rtgiu", queries, key_new, preferred_element_type=jnp.float32)
        * scale_factor
    )
    token_ids = jnp.arange(queries.shape[1], dtype=jnp.int32)
    causal = token_ids[:, None] >= token_ids[None, :]
    scores_new = jnp.where(causal[None, :, None, None, :], scores_new, -1e30)
    highest = jnp.maximum(jnp.max(scores_old, axis=-1), jnp.max(scores_new, axis=-1))
    expo_old = jnp.exp(scores_old - highest[..., None])
    expo_new = jnp.exp(scores_new - highest[..., None])
    denominator = jnp.sum(expo_old, axis=-1) + jnp.sum(expo_new, axis=-1)
    weight_old = (expo_old / denominator[..., None]).astype(jnp.bfloat16)
    weight_new = (expo_new / denominator[..., None]).astype(jnp.bfloat16)
    attended = jnp.einsum(
        "rtgis,rsgd->rtgid", weight_old, cache_rows[:, :, 1], preferred_element_type=jnp.float32
    )
    attended = attended + jnp.einsum(
        "rtgiu,rugd->rtgid", weight_new, value_new, preferred_element_type=jnp.float32
    )
    return attended.astype(jnp.bfloat16)


def hop(source, target, sends, arrivals, place):
    return pltpu.make_async_remote_copy(
        src_ref=source,
        dst_ref=target,
        send_sem=sends,
        recv_sem=arrivals,
        device_id=place,
        device_id_type=pl.DeviceIdType.MESH,
    )


def block_kernel(
    head_devices,
    places,
    tokens_ref,
    gain_ref,
    qkv_ref,
    out_weight_ref,
    cache_ref,
    lengths_ref,
    positions_ref,
    out_ref,
    tok,
    gain,
    gain_wide,
    left,
    ring,
    chunk,
    weights,
    own_sum,
    core_send,
    core_recv,
    row_send,
    row_recv,
    square_all,
    square_core,
    square_mid,
    square_recv,
    query_buf,
    attended_buf,
    attended_send,
    attended_recv,
    part_send,
    part_recv,
    part_own,
    load_sems,
    ring_sems,
    tile_sems,
    weight_sems,
    core_sems,
    row_sends,
    row_recvs,
    square_sems,
    att_sends,
    att_recvs,
    pair_sends,
    pair_recvs,
    part_sends,
    part_recvs,
):
    f32, bf16 = jnp.float32, jnp.bfloat16
    rows_total, pair, local_width = tokens_ref.shape
    total_tokens = rows_total * pair
    columns, head_dim = qkv_ref.shape[1], qkv_ref.shape[3]
    groups = qkv_ref.shape[2]
    group_size = columns - 2
    pieces = columns // 2
    slots = ring.shape[0]
    max_len = (cache_ref.shape[0] // (2 * groups * head_devices)) // lengths_ref.shape[0]
    rows_local = lengths_ref.shape[0]
    all_groups = groups * head_devices
    near = rows_local * pair
    block = groups * near
    lanes = places // 2
    team = lanes * head_devices
    contraction = local_width * groups
    width = lax.axis_index("gx")
    head = lax.axis_index("gy")
    core = lax.rem(width, 2)
    lane_at = width // 2
    mine = lane_at * head_devices + head
    source_at = width * head_devices + head
    partner = {"gx": width + 1 - 2 * core}

    def member(off):
        other = lax.rem(mine + off, team)
        far_lane, far_head = other // head_devices, lax.rem(other, head_devices)
        return other, {"gx": far_lane * 2 + core, "gy": far_head}

    def bring(piece, slot):
        return [
            pltpu.make_async_copy(
                qkv_ref.at[:, piece * 2 + at], ring.at[slot, at], ring_sems.at[slot, at]
            )
            for at in range(2)
        ]

    load_tokens = pltpu.make_async_copy(
        tokens_ref.reshape(total_tokens, local_width), tok, load_sems.at[0]
    )
    load_gain = pltpu.make_async_copy(gain_ref, gain, load_sems.at[1])
    load_tokens.start()
    load_gain.start()
    for piece in range(min(slots, pieces)):
        for copy in bring(piece, piece):
            copy.start()
    barrier = pltpu.get_barrier_semaphore()
    pl.semaphore_signal(barrier, inc=1, device_id=partner, device_id_type=pl.DeviceIdType.MESH)
    for off in range(1, team):
        pl.semaphore_signal(
            barrier, inc=1, device_id=member(off)[1], device_id_type=pl.DeviceIdType.MESH
        )

    made = lax.broadcasted_iota(jnp.int32, (total_tokens * groups, total_tokens), 0)
    held = lax.broadcasted_iota(jnp.int32, (total_tokens * groups, total_tokens), 1)
    target = made // block
    owner_core = target // team
    owner_lane = lax.rem(target, team) // head_devices
    owner_head = lax.rem(target, head_devices)
    owner = (owner_lane * 2 + owner_core) * head_devices + owner_head
    chosen = owner * near + lax.rem(made, near) == held
    chooser = jnp.where(chosen, 1.0, 0.0)
    group_row = lax.rem(
        lax.broadcasted_iota(jnp.int32, (total_tokens * groups, 128), 0), block
    ) // near
    feature = lax.broadcasted_iota(jnp.int32, (128 * groups, 128 * groups), 0)
    goal = lax.broadcasted_iota(jnp.int32, (128 * groups, 128 * groups), 1)
    spread = jnp.where(
        goal == lax.rem(feature, 128) * groups + feature // 128, 1.0, 0.0
    ).astype(bf16)

    load_tokens.wait()
    load_gain.wait()
    gain_wide[...] = gain[...].astype(f32)
    depth = 1024

    def widen(at, squares):
        start = pl.multiple_of(at * depth, depth)
        wide = tok[:, pl.ds(start, depth)].astype(f32)
        scale = jnp.concatenate(
            [gain_wide[pl.ds(at * (depth // 128) + q, 1), :] for q in range(depth // 128)], axis=1
        )
        hidden = (wide * scale).astype(bf16)
        ordered = jnp.dot(chooser.astype(bf16), hidden, preferred_element_type=f32)
        for q in range(depth // 128):
            part = wide[:, q * 128 : (q + 1) * 128]
            squares += part * part
            near_part = ordered[:, q * 128 : (q + 1) * 128]
            split = jnp.concatenate(
                [jnp.where(group_row == group, near_part, 0.0) for group in range(groups)], axis=1
            ).astype(bf16)
            begin = pl.multiple_of((start + q * 128) * groups, 128 * groups)
            left[:, pl.ds(begin, 128 * groups)] = jnp.dot(
                split, spread, preferred_element_type=f32
            ).astype(bf16)
        return squares

    squares = lax.fori_loop(
        0, local_width // depth, widen, jnp.zeros((total_tokens, 128), f32)
    )
    square_all[...] = jnp.dot(
        chooser, squares, preferred_element_type=f32, precision=lax.Precision.HIGHEST
    ).reshape(square_all.shape)
    pl.semaphore_wait(barrier, team)

    square_hop = hop(
        square_all.at[1 - core], square_core, square_sems.at[0], square_sems.at[1], partner
    )
    square_hop.start()

    def core_hop(piece):
        return hop(
            core_send.at[piece],
            core_recv.at[piece],
            core_sems.at[0, piece],
            core_sems.at[1, piece],
            partner,
        )

    def row_hop(piece, off):
        other, place = member(off)
        return hop(
            row_send.at[piece, other],
            row_recv.at[piece, mine],
            row_sends.at[piece, other],
            row_recvs.at[piece, mine],
            place,
        )

    def row_arrival(piece, off):
        other, place = member(off)
        return hop(
            row_send.at[piece, other],
            row_recv.at[piece, other],
            row_sends.at[piece, other],
            row_recvs.at[piece, other],
            place,
        )

    def pass_on(piece):
        core_hop(piece).wait_recv()
        total = own_sum[lax.rem(piece, 3), core] + core_recv[piece].astype(f32)
        row_send[piece] = total.reshape(row_send.shape[1:]).astype(bf16)
        row_recv[piece, mine] = row_send[piece, mine]
        for off in range(1, team):
            row_hop(piece, off).start()

    def weight_copy(at):
        across = part_own.shape[2]
        return pltpu.make_async_copy(
            out_weight_ref.at[:, pl.ds(at * across, across)],
            weights.at[:, pl.ds(at * across, across)],
            weight_sems.at[at],
        )

    stretches = part_own.shape[0]
    cache_slot, cached_slot = pieces % 2, (pieces - 1) % 2
    cache_rows = cache_ref.shape[0]
    load_cache = pltpu.make_async_copy(
        cache_ref, chunk.at[cache_slot, pl.ds(0, cache_rows)], load_sems.at[3]
    )

    @pl.loop(0, pieces)
    def _(piece):
        slot, here = lax.rem(piece, slots), lax.rem(piece, 2)

        @pl.when(piece == pieces - 1)
        def _():
            load_cache.start()

        for copy in bring(piece, slot):
            copy.wait()
        flat = ring.reshape(slots, 2, contraction, head_dim)
        moves = [
            pltpu.make_async_copy(
                flat.at[slot, at],
                chunk.at[here, pl.ds(at * contraction, contraction)],
                tile_sems.at[at],
            )
            for at in range(2)
        ]
        for move in moves:
            move.start()

        for move in moves:
            move.wait()

        @pl.when(piece + slots < pieces)
        def _():
            for copy in bring(piece + slots, slot):
                copy.start()

        right = jnp.concatenate(
            [chunk[here, pl.ds(0, contraction)], chunk[here, pl.ds(contraction, contraction)]], axis=1
        )
        total = jnp.dot(left[...], right, preferred_element_type=f32)
        kept = lax.rem(piece, 3)
        own_sum[kept] = total.reshape(own_sum.shape[1:])
        core_send[piece] = own_sum[kept, 1 - core].astype(bf16)
        core_hop(piece).start()

        @pl.when(piece >= 2)
        def _():
            pass_on(piece - 2)

    pass_on(pieces - 2)
    pass_on(pieces - 1)
    square_hop.wait_recv()
    square_mid[...] = (square_all[core] + square_core[...]).reshape(square_mid.shape)
    square_recv[lane_at] = square_mid[mine]

    def square_send(off):
        other_lane = lax.rem(lane_at + off, lanes)
        return hop(
            square_mid.at[other_lane * head_devices + head],
            square_recv.at[lane_at],
            square_sems.at[2 + 2 * off],
            square_sems.at[3 + 2 * off],
            {"gx": other_lane * 2 + core},
        )

    def square_arrival(off):
        other_lane = lax.rem(lane_at + lanes - off, lanes)
        return hop(
            square_mid.at[mine],
            square_recv.at[other_lane],
            square_sems.at[2 + 2 * off],
            square_sems.at[3 + 2 * off],
            {"gx": other_lane * 2 + core},
        )

    for off in range(1, lanes):
        square_send(off).start()
    early = stretches - stretches // 4
    for at in range(early):
        weight_copy(at).start()

    stride = max_len + 16
    steps = 16
    kinds = 2 * all_groups
    size = steps * kinds
    to_row = lax.broadcasted_iota(jnp.int32, (size, size), 0)
    from_row = lax.broadcasted_iota(jnp.int32, (size, size), 1)
    regroup = jnp.where(
        from_row == lax.rem(to_row, steps) * kinds + to_row // steps, 1.0, 0.0
    ).astype(bf16)
    load_cache.wait()
    for row in range(rows_local):

        @pl.loop(0, max_len // (2 * steps))
        def _(step):
            first = pl.multiple_of(row * max_len * kinds + step * 2 * size, size)
            both = jnp.concatenate(
                [chunk[cache_slot, pl.ds(first, size)], chunk[cache_slot, pl.ds(first + size, size)]],
                axis=1,
            )
            sorted_rows = jnp.dot(regroup, both, preferred_element_type=f32).astype(bf16)
            for kind in range(kinds):
                base = (row * kinds + kind) * stride
                for half in range(2):
                    at = pl.multiple_of(base + (step * 2 + half) * steps, 16)
                    chunk[cached_slot, pl.ds(at, steps)] = sorted_rows[
                        kind * steps : (kind + 1) * steps, half * head_dim : (half + 1) * head_dim
                    ]

    row_at = lax.broadcasted_iota(jnp.int32, (block, head_dim), 0)
    lane = lax.broadcasted_iota(jnp.int32, (block, head_dim), 1)
    half_dim = head_dim // 2
    place = jnp.zeros((block, head_dim), jnp.int32)
    for row in range(rows_local):
        place = jnp.where(
            lax.rem(row_at, near) // pair == row, positions_ref[source_at * rows_local + row], place
        )
    place = (place + lax.rem(row_at, pair)).astype(f32)
    index_half = lax.rem(lane, half_dim).astype(f32)
    frequency = jnp.exp(index_half * (-2.0 * math.log(rope_base) / head_dim))
    angles = place * frequency
    cosine = jnp.cos(angles)
    sine = jnp.where(lane < half_dim, -jnp.sin(angles), jnp.sin(angles))

    for off in range(1, lanes):
        square_arrival(off).wait_recv()
    square_total = square_recv[0]
    for at in range(1, lanes):
        square_total = square_total + square_recv[at]
    inv_rms = lax.rsqrt(
        jnp.sum(square_total, axis=1, keepdims=True) / (local_width * places) + norm_eps
    )

    @pl.loop(0, pieces)
    def _(piece):
        for off in range(1, team):
            row_arrival(piece, off).wait_recv()

    small = lax.broadcasted_iota(jnp.int32, (block, head_dim), 0)
    scale_factor = 1.0 / math.sqrt(head_dim)
    count = pair * group_size
    slot_id = lax.broadcasted_iota(jnp.int32, (count, stride), 1)
    token_id = lax.broadcasted_iota(jnp.int32, (count, stride), 0) // group_size
    fresh_seen = (slot_id >= max_len) & (slot_id - max_len <= token_id)

    def send_to(far, at):
        other = at * head_devices + far

        @pl.when(other != mine)
        def _():
            hop(
                attended_send.at[far],
                attended_recv.at[source_at],
                att_sends.at[other],
                att_recvs.at[mine],
                {"gx": at * 2 + core, "gy": far},
            ).start()

        @pl.when(other == mine)
        def _():
            attended_recv[source_at] = attended_send[far]

    ends = [
        far
        for near_end in range((head_devices + 1) // 2)
        for far in sorted({near_end, head_devices - 1 - near_end})
    ]
    for far in ends:
        for column in range(columns):
            piece, side = column // 2, column % 2
            value = row_recv[piece, far, :, side * head_dim : (side + 1) * head_dim].astype(f32)
            for at in range(1, lanes):
                value = value + row_recv[
                    piece, at * head_devices + far, :, side * head_dim : (side + 1) * head_dim
                ].astype(f32)
            value = value * inv_rms
            if column <= group_size:
                turned = jnp.concatenate([value[:, half_dim:], value[:, :half_dim]], axis=1)
                value = value * cosine + turned * sine
            if column < group_size:
                query_buf[far, column * block : (column + 1) * block, :] = value
            else:
                kind = column - group_size
                for group in range(groups):
                    for row in range(rows_local):
                        start = group * near + row * pair
                        moved = pltpu.roll(value, (block - start) % block, 0) if start else value
                        fresh = jnp.where(small < pair, moved, 0.0)
                        base = (
                            row * kinds + kind * all_groups + far * groups + group
                        ) * stride + max_len
                        chunk[cached_slot, pl.ds(base, 16)] = jnp.concatenate(
                            [fresh, jnp.zeros((16 - block, head_dim), f32)], axis=0
                        ).astype(bf16)
        for row in range(rows_local):
            seen = (slot_id < lengths_ref[row]) | fresh_seen
            for group in range(groups):
                every = far * groups + group
                first = group * near + row * pair
                queries = jnp.concatenate(
                    [
                        query_buf[far, pl.ds(first + token, group_size, stride=block), :]
                        for token in range(pair)
                    ],
                    axis=0,
                ).astype(bf16)
                keys = chunk[cached_slot, pl.ds((row * kinds + every) * stride, stride)]
                values = chunk[
                    cached_slot, pl.ds((row * kinds + all_groups + every) * stride, stride)
                ]
                scores = lax.dot_general(
                    queries, keys, (((1,), (1,)), ((), ())), preferred_element_type=f32
                )
                scores = jnp.where(seen, scores * scale_factor, -1e30)
                expo = jnp.exp(scores - jnp.max(scores, axis=1, keepdims=True))
                weight = (expo / jnp.sum(expo, axis=1, keepdims=True)).astype(bf16)
                result = jnp.dot(weight, values, preferred_element_type=f32)
                for token in range(pair):
                    attended_buf[far, pl.ds(first + token, group_size, stride=block), :] = result[
                        token * group_size : (token + 1) * group_size
                    ]
        for at in range(group_size):
            attended_send[far, :, at * head_dim : (at + 1) * head_dim] = attended_buf[
                far, at * block : (at + 1) * block, :
            ].astype(bf16)
        for at in range(lanes):
            send_to(far, at)

    def att_hop(off):
        other, place_of = member(off)
        return hop(
            attended_send.at[place_of["gy"]],
            attended_recv.at[source_at],
            att_sends.at[other],
            att_recvs.at[mine],
            place_of,
        )

    def source_of(other, which):
        return ((other // head_devices) * 2 + which) * head_devices + lax.rem(other, head_devices)

    def att_arrival(off):
        other, place_of = member(off)
        return hop(
            attended_send.at[place_of["gy"]],
            attended_recv.at[source_of(other, core)],
            att_sends.at[other],
            att_recvs.at[other],
            place_of,
        )

    def pair_hop(other, which):
        from_at = source_of(other, which)
        return hop(
            attended_recv.at[from_at],
            attended_recv.at[from_at],
            pair_sends.at[other],
            pair_recvs.at[other],
            partner,
        )

    pair_hop(mine, core).start()
    later = iter(range(early, stretches))
    for off in range(1, team):
        for at in itertools.islice(later, 2):
            weight_copy(at).start()
        att_arrival(off).wait_recv()
        pair_hop(lax.rem(mine + off, team), core).start()
    for at in later:
        weight_copy(at).start()
    for off in range(team):
        pair_hop(lax.rem(mine + off, team), 1 - core).wait_recv()

    heads_width = group_size * head_dim
    sources = places * head_devices
    first_rows = lax.rem(lax.broadcasted_iota(jnp.int32, (2 * block, heads_width), 0), block) // near
    for at in range(0, sources, 2):
        both = jnp.concatenate([attended_recv[at], attended_recv[at + 1]], axis=0).astype(f32)
        for group in range(groups):
            left[at * block : (at + 2) * block, group * heads_width : (group + 1) * heads_width] = (
                jnp.where(first_rows == group, both, 0.0).astype(bf16)
            )

    def part_hop(at, off):
        other = lax.rem(head + off, head_devices)
        return hop(
            part_send.at[at, other],
            part_recv.at[at, head],
            part_sends.at[at, other],
            part_recvs.at[at, head],
            {"gy": other},
        )

    def part_arrival(at, off):
        other = lax.rem(head + off, head_devices)
        return hop(
            part_send.at[at, other],
            part_recv.at[at, other],
            part_sends.at[at, other],
            part_recvs.at[at, other],
            {"gy": other},
        )

    across = part_own.shape[2]
    share = total_tokens // head_devices

    @pl.loop(0, stretches)
    def _(at):
        weight_copy(at).wait()
        span = pl.ds(pl.multiple_of(at * across, across), across)
        product = jnp.dot(
            left[:, : groups * heads_width], weights[:, span], preferred_element_type=f32
        )
        upper = lax.broadcasted_iota(jnp.int32, (block, across), 0) < near
        tiles = []
        for source in range(sources):
            tile = product[source * block : (source + 1) * block]
            tiles.append(tile + pltpu.roll(tile, near, 0))
        joined = [
            jnp.where(upper, tiles[source], tiles[source + 1]) for source in range(0, sources, 2)
        ]
        per = len(joined) // head_devices
        for far in range(head_devices):
            value = jnp.concatenate(joined[far * per : (far + 1) * per], axis=0)
            part_send[at, far] = value.astype(bf16)

            @pl.when(far == head)
            def _():
                part_own[at] = value

        for off in range(1, head_devices):
            part_hop(at, off).start()

    mine_rows = pl.ds(pl.multiple_of(head * share, share), share)

    @pl.loop(0, stretches)
    def _(at):
        span = pl.ds(pl.multiple_of(at * across, across), across)
        value = part_own[at] + tok[mine_rows, span].astype(f32)
        for off in range(1, head_devices):
            part_arrival(at, off).wait_recv()
            value = value + part_recv[at, lax.rem(head + off, head_devices)].astype(f32)
        for row in range(share // pair):
            for tile in range(across // 128):
                out_ref[row, at * (across // 128) + tile] = value[
                    row * pair : (row + 1) * pair, tile * 128 : (tile + 1) * 128
                ]

    square_hop.wait_send()
    for off in range(1, lanes):
        square_send(off).wait_send()

    @pl.loop(0, pieces)
    def _(piece):
        core_hop(piece).wait_send()
        for off in range(1, team):
            row_hop(piece, off).wait_send()

    for off in range(1, team):
        att_hop(off).wait_send()
    for off in range(team):
        pair_hop(lax.rem(mine + off, team), core).wait_send()

    @pl.loop(0, stretches)
    def _(at):
        for off in range(1, head_devices):
            part_hop(at, off).wait_send()


def store_kernel(value_ref, out_ref, sem):
    copy = pltpu.make_async_copy(value_ref, out_ref, sem.at[0])
    copy.start()
    copy.wait()


def whole_block(tokens, norm_gain, qkv_weight, out_weight, kv_cache, lengths, positions):
    f32, bf16 = jnp.float32, jnp.bfloat16
    rows_total, pair, local_width = tokens.shape
    groups, columns, head_dim = qkv_weight.shape[1:]
    places, head_devices = lax.axis_size("gx"), lax.axis_size("gy")
    rows_local, max_len = kv_cache.shape[:2]
    total_tokens = rows_total * pair
    group_size = columns - 2
    pieces = columns // 2
    slots = 3
    lanes = places // 2
    team = lanes * head_devices
    block = groups * rows_local * pair
    sources = places * head_devices
    share = total_tokens // head_devices
    across = 512
    stretches = local_width // across
    contraction = local_width * groups
    wide = 2 * head_dim
    hbm = pl.BlockSpec(memory_space=pl.ANY)
    smem = pl.BlockSpec(memory_space=pltpu.SMEM)
    dma = pltpu.SemaphoreType.DMA
    got = pl.pallas_call(
        functools.partial(block_kernel, head_devices, places),
        out_shape=jax.ShapeDtypeStruct((share // pair, local_width // 128, pair, 128), f32),
        in_specs=[hbm, hbm, hbm, hbm, hbm, smem, smem],
        out_specs=pl.BlockSpec(memory_space=pltpu.VMEM),
        scratch_shapes=[
            pltpu.VMEM((total_tokens, local_width), bf16),
            pltpu.VMEM((local_width // 128, 128), bf16),
            pltpu.VMEM((local_width // 128, 128), f32),
            pltpu.VMEM((total_tokens * groups, contraction), bf16),
            pltpu.VMEM((slots, 2, local_width, groups, head_dim), bf16),
            pltpu.VMEM((2, 2 * contraction, head_dim), bf16),
            pltpu.VMEM((out_weight.shape[0] * head_dim, local_width), bf16),
            pltpu.VMEM((3, 2, team * block, wide), f32),
            pltpu.VMEM((pieces, team * block, wide), bf16),
            pltpu.VMEM((pieces, team * block, wide), bf16),
            pltpu.VMEM((pieces, team, block, wide), bf16),
            pltpu.VMEM((pieces, team, block, wide), bf16),
            pltpu.VMEM((2, team * block, 128), f32),
            pltpu.VMEM((team * block, 128), f32),
            pltpu.VMEM((team, block, 128), f32),
            pltpu.VMEM((lanes, block, 128), f32),
            pltpu.VMEM((head_devices, group_size * block, head_dim), f32),
            pltpu.VMEM((head_devices, group_size * block, head_dim), f32),
            pltpu.VMEM((head_devices, block, group_size * head_dim), bf16),
            pltpu.VMEM((sources, block, group_size * head_dim), bf16),
            pltpu.VMEM((stretches, head_devices, share, across), bf16),
            pltpu.VMEM((stretches, head_devices, share, across), bf16),
            pltpu.VMEM((stretches, share, across), f32),
            dma((4,)),
            dma((slots, 2)),
            dma((2,)),
            dma((stretches,)),
            dma((2, pieces)),
            dma((pieces, team)),
            dma((pieces, team)),
            dma((2 + 2 * lanes,)),
            dma((team,)),
            dma((team,)),
            dma((team,)),
            dma((team,)),
            dma((stretches, head_devices)),
            dma((stretches, head_devices)),
        ],
        compiler_params=pltpu.CompilerParams(
            collective_id=0, has_side_effects=True, vmem_limit_bytes=60 << 20
        ),
    )(
        tokens,
        norm_gain.reshape(-1, 128),
        jnp.transpose(qkv_weight, (0, 2, 1, 3)),
        out_weight.reshape(-1, local_width),
        kv_cache.reshape(-1, head_dim),
        lengths,
        positions,
    )
    got = pl.pallas_call(
        store_kernel,
        out_shape=jax.ShapeDtypeStruct(got.shape, f32),
        in_specs=[pl.BlockSpec(memory_space=pltpu.VMEM)],
        out_specs=hbm,
        scratch_shapes=[dma((1,))],
    )(got)
    return jnp.transpose(got, (0, 2, 1, 3)).reshape(share // pair, pair, local_width)


def body(tokens, norm_gain, qkv_weight, out_weight, kv_cache, lengths, positions):
    rows_local = kv_cache.shape[0]
    head_devices = lax.axis_size("gy")
    width_index = lax.axis_index("gx")
    head_index = lax.axis_index("gy")
    total_rows = tokens.shape[0]
    local_width = tokens.shape[2]
    groups_local = qkv_weight.shape[1]
    group_width = qkv_weight.shape[2]
    head_dim = qkv_weight.shape[3]
    group_size = group_width - 2
    block_rows = rows_local * head_devices
    places = lax.axis_size("gx")
    pair = tokens.shape[1]
    contraction = local_width * groups_local
    resident = (
        out_weight.size
        + 10 * contraction * head_dim
        + total_rows * pair * (2 * local_width + groups_local * contraction)
    )
    if (
        groups_local * rows_local * pair == 8
        and places % 2 == 0
        and head_devices > 1
        and total_rows == rows_local * places * head_devices
        and places % head_devices == 0
        and group_width % 2 == 0
        and head_dim == 128
        and kv_cache.shape[1] % 32 == 0
        and local_width % 1024 == 0
        and 2 * resident < 59 << 20
    ):
        return whole_block(
            tokens, norm_gain, qkv_weight, out_weight, kv_cache, lengths, positions
        )
    tokens_wide = tokens.astype(jnp.float32)
    hidden = (tokens_wide * norm_gain.astype(jnp.float32)).astype(jnp.bfloat16)
    squares = jnp.sum(tokens_wide * tokens_wide, axis=-1)
    partial_value = jnp.dot(
        hidden.reshape(total_rows * 2, local_width),
        qkv_weight.reshape(local_width, -1),
        preferred_element_type=jnp.float32,
    )
    partial_value = partial_value.reshape(total_rows, 2, groups_local, group_width, head_dim)
    block_sum, block_squares = (
        lax.psum_scatter(partial_value, "gx", scatter_dimension=0, tiled=True),
        lax.psum_scatter(squares, "gx", scatter_dimension=0, tiled=True),
    )
    inv_rms = lax.rsqrt(block_squares / D + norm_eps)
    ready = finish(
        block_sum * inv_rms[:, :, None, None, None], positions, width_index * block_rows, block_rows
    )
    packed = lax.all_to_all(ready, "gy", split_axis=0, concat_axis=2, tiled=True)
    queries = packed[:, :, :, :group_size]
    key_new = packed[:, :, :, group_size]
    value_new = packed[:, :, :, group_size + 1]
    attended = attend(queries, key_new, value_new, kv_cache, lengths)
    regrouped = lax.all_to_all(attended, "gy", split_axis=2, concat_axis=0, tiled=True)
    out_flat = out_weight.reshape(-1, local_width)
    row_piece = lax.all_gather(regrouped, "gx", axis=0, tiled=True)
    piece_rows = row_piece.shape[0]
    product = jnp.dot(
        row_piece.reshape(piece_rows * 2, -1), out_flat, preferred_element_type=jnp.float32
    )
    terms = product.astype(jnp.bfloat16).reshape(head_devices, -1, 2, local_width)
    arrived = lax.all_to_all(terms, "gy", split_axis=0, concat_axis=0)
    own_sum = jnp.sum(arrived.astype(jnp.float32), axis=0)
    row_share = total_rows // head_devices
    residual = lax.dynamic_slice_in_dim(tokens, head_index * row_share, row_share, 0).astype(
        jnp.float32
    )
    return residual + own_sum


def solution(mesh):
    return jax.shard_map(
        body,
        mesh=mesh,
        in_specs=(
            P("groups", None, "gx"),
            P("gx"),
            P("gx", "gy", None, None),
            P("gy", None, "gx"),
            P(("groups", "gx", "gy"), None, None, None, None),
            P(("groups", "gx", "gy")),
            P("groups"),
        ),
        out_specs=P(("groups", "gy"), None, "gx"),
        check_vma=False,
    )
```
